32 devices in a mesh: gx: 2 (over y), gy: 4 (over z), gz: 4 (over x, core).
Axes of the slice: x: 2, y: 2, z: 4, core: 2. Of those that a mesh axis runs over, the one named last changes fastest.
Arguments:
- solution: float32 [56, 9, 4096], P(None, None, ('gx', 'gy', 'gz')), may hold values from -6 to 6
- jacobians: float32 [3, 9, 9, 4096], P(None, None, None, ('gx', 'gy', 'gz')), may hold values from -2 to 2
- derivative_stiffness: float32 [3, 56, 56], replicated, may hold values from -0.75 to 0.75
- volume_stiffness: float32 [3, 56, 56], replicated, may hold values from -0.375 to 0.375
- face_project: float32 [4, 21, 56], replicated, may hold values from -0.75 to 0.75
- face_lift: float32 [4, 56, 21], replicated, may hold values from -0.625 to 0.625
- face_rotation: float32 [3, 21, 21], replicated, may hold values from -1.25 to 1.25
- local_solver: float32 [4, 9, 9, 4096], P(None, None, None, ('gx', 'gy', 'gz')), may hold values from -2 to 2
- neighbour_solver: float32 [4, 9, 9, 4096], P(None, None, None, ('gx', 'gy', 'gz')), may hold values from -2 to 2
- cluster: int32 [4096], P(('gx', 'gy', 'gz')), may hold values from 0 to 2
- neighbours: int32 [4, 4096], P(None, ('gx', 'gy', 'gz')), may hold values from 0 to 1279, as said below
- orient: int32 [4, 4096], P(None, ('gx', 'gy', 'gz')), may hold values from 0 to 2
- send_faces: int32 [6, 4096], P(None, ('gx', 'gy', 'gz')), may hold values from 0 to 511
- counts: int32 [6, 32], P(None, ('gx', 'gy', 'gz')), may hold values from 64 to 128, as said below
Outputs:
- advanced: float32 [56, 9, 4096], P(None, None, ('gx', 'gy', 'gz'))
The draws below stay inside these ranges and needn't reach their ends.
Inputs may be any that keep to these rules, and one draw needn't show every extreme that they name: `neighbours`: below 512 a value names a face of the own partition; above, a slot of the blocks of one direction whose index is below the sending partition's count for that list. `send_faces`: each value is a local face j * 128 + n of the sending partition. `counts`: entry [k, p] is how many leading slots of partition p's list k are used; some entry equals 128.
All inputs are finite; a program needn't handle non-finite values.
Results may differ from the reference program's by a relative error of at most 0.0001.
Values sent between devices are 32-bit elements; how exact they have to be, the bound alone decides.
No kernel may reach another device: no remote copies, remote signals or barrier semaphores. Data moves between devices by JAX's collectives and lax.ppermute only.
A program may use at most 64 MiB of HBM per device.

```python
import math
import jax
import jax.numpy as jnp
from jax import lax

E_DEV = 128
SLOTS = 128
BASIS = 56
QUANTITIES = 9
FACE_BASIS = 21
DERIVATIVES = 6
SUBSTEPS = 4
ELEMENTS = 4096
N_GX = 2
N_GY = 4
N_GZ = 4
DEVICES = 32


def block_counts(key):
    base_key = jax.random.fold_in(key, 7)
    lowest_count = (SLOTS + 1) // 2
    drawn = jax.random.randint(jax.random.fold_in(base_key, 1), (6 * DEVICES,), lowest_count, SLOTS + 1)
    chosen_entry = jax.random.randint(jax.random.fold_in(base_key, 2), (), 0, 6 * DEVICES)
    drawn = jnp.where(jnp.arange(6 * DEVICES, dtype=jnp.int32) == chosen_entry, SLOTS, drawn)
    return drawn.reshape(6, DEVICES).astype(jnp.int32)


def draw_counts(key, part):
    return block_counts(key)


def draw_neighbours(key, part):
    grid_counts = block_counts(key).reshape(6, N_GX, N_GY, N_GZ)
    received = jnp.stack([jnp.roll(grid_counts[0], 1, 0), jnp.roll(grid_counts[1], -1, 0), jnp.roll(grid_counts[2], 1, 1), jnp.roll(grid_counts[3], -1, 1), jnp.roll(grid_counts[4], 1, 2), jnp.roll(grid_counts[5], -1, 2)]).reshape(6, DEVICES)
    element_total = E_DEV * DEVICES
    owner_device = jnp.arange(element_total, dtype=jnp.int32) // E_DEV
    own_key = jax.random.fold_in(key, 9)
    inner_face = jax.random.randint(jax.random.fold_in(own_key, 1), (4, element_total), 0, 4 * E_DEV)
    direction = jax.random.randint(jax.random.fold_in(own_key, 2), (4, element_total), 0, 6)
    limit = received[direction, jnp.broadcast_to(owner_device[None, :], (4, element_total))]
    slot_index = jax.random.randint(jax.random.fold_in(own_key, 3), (4, element_total), 0, limit)
    is_ghost = jax.random.randint(jax.random.fold_in(own_key, 4), (4, element_total), 0, 4) == 0
    ghost_value = 4 * E_DEV + direction * SLOTS + slot_index
    return jnp.where(is_ghost, ghost_value, inner_face).astype(jnp.int32)


def with_ends(values, key, low, top_value):
    shape = values.shape
    place = [jax.random.randint(jax.random.fold_in(key, axis), (), 0, shape[axis]) for axis in range(len(shape))]
    values = values.at[tuple(place)].set(low)
    longest = shape.index(max(shape))
    place[longest] = (place[longest] + 1) % shape[longest]
    return values.at[tuple(place)].set(top_value)


def level_of(stream_key, extent, split, least, largest):
    def one(axis_at, shards_of):
        draws = jax.random.uniform(jax.random.fold_in(jax.random.fold_in(stream_key, 6), axis_at), (shards_of,), jnp.float32, least / len(split), largest / len(split))
        return jnp.repeat(jnp.exp(draws), extent[axis_at] // shards_of).reshape((-1,) + (1,) * (len(extent) - axis_at - 1))

    level = one(*split[0])
    for cut in split[1:]:
        level = level * one(*cut)
    return level


def gaussian(key, dims, spread, most, split=(), held_as=jnp.bfloat16):
    level = level_of(key, dims, split, -0.22, 0.18) if split else 1.0
    values = jax.random.normal(key, dims, jnp.float32) * spread * level
    return jnp.minimum(jnp.maximum(values, -most), most).astype(held_as)


def setup_inputs(seed: int = 0) -> dict:
    key_of = jax.random.split(jax.random.key(seed), 15)
    return {
        "solution": gaussian(key_of[0], (BASIS, QUANTITIES, ELEMENTS), 1.0, 6.0, ((2, 32),), jnp.float32),
        "jacobians": gaussian(key_of[1], (3, QUANTITIES, QUANTITIES, ELEMENTS), 7 ** -0.5, 2.0, ((3, 32),), jnp.float32),
        "derivative_stiffness": gaussian(key_of[2], (3, BASIS, BASIS), BASIS ** -0.5, 0.75, (), jnp.float32),
        "volume_stiffness": gaussian(key_of[3], (3, BASIS, BASIS), (4 * BASIS) ** -0.5, 0.375, (), jnp.float32),
        "face_project": gaussian(key_of[4], (4, FACE_BASIS, BASIS), BASIS ** -0.5, 0.75, (), jnp.float32),
        "face_lift": gaussian(key_of[5], (4, BASIS, FACE_BASIS), (4 * FACE_BASIS) ** -0.5, 0.625, (), jnp.float32),
        "face_rotation": gaussian(key_of[6], (3, FACE_BASIS, FACE_BASIS), FACE_BASIS ** -0.5, 1.25, (), jnp.float32),
        "local_solver": gaussian(key_of[7], (4, QUANTITIES, QUANTITIES, ELEMENTS), QUANTITIES ** -0.5, 2.0, ((3, 32),), jnp.float32),
        "neighbour_solver": gaussian(key_of[8], (4, QUANTITIES, QUANTITIES, ELEMENTS), QUANTITIES ** -0.5, 2.0, ((3, 32),), jnp.float32),
        "cluster": with_ends(jax.random.randint(key_of[9], (ELEMENTS,), 0, 3), jax.random.fold_in(key_of[9], 1), 0, 2).astype(jnp.int32),
        "neighbours": draw_neighbours(jax.random.fold_in(key_of[14], 71), 0),
        "orient": with_ends(jax.random.randint(key_of[11], (4, ELEMENTS), 0, 3), jax.random.fold_in(key_of[11], 1), 0, 2).astype(jnp.int32),
        "send_faces": with_ends(jax.random.randint(key_of[12], (6, SLOTS * DEVICES), 0, 4 * E_DEV), jax.random.fold_in(key_of[12], 1), 0, (4 * E_DEV) - 1).astype(jnp.int32),
        "counts": draw_counts(jax.random.fold_in(key_of[14], 71), 0),
    }


highest = lax.Precision.HIGHEST
coarse_span = 1.0


def derivative_terms(solution, jacobians, stiff_stack):
    current = solution
    results = [solution]
    for power_index in range(DERIVATIVES - 1):
        mixed_terms = jnp.dot(stiff_stack, current.reshape(BASIS, -1), precision=highest).reshape(3, BASIS, QUANTITIES, -1)
        current = -jnp.einsum("dkqe,dqpe->kpe", mixed_terms, jacobians, precision=highest)
        results.append(current)
    return results


def time_weights(cluster, substep):
    period = jnp.left_shift(jnp.ones_like(cluster), cluster)
    offset = (substep % period).astype(jnp.float32)
    finish = ((substep + 1) % period) == 0
    substep_span = coarse_span / SUBSTEPS
    upper_time = (offset + 1.0) * substep_span
    lower_time = offset * substep_span
    weight_rows = [(upper_time ** (power_index + 1) - lower_time ** (power_index + 1)) / math.factorial(power_index + 1) for power_index in range(DERIVATIVES)]
    return jnp.stack(weight_rows), finish


def volume_term(accumulated, jacobians, volume_stack):
    mixed_terms = jnp.dot(volume_stack, accumulated.reshape(BASIS, -1), precision=highest).reshape(3, BASIS, QUANTITIES, -1)
    return jnp.einsum("dkqe,dqpe->kpe", mixed_terms, jacobians, precision=highest)


def reference(solution, jacobians, derivative_stiffness, volume_stiffness, face_project, face_lift, face_rotation, local_solver, neighbour_solver, cluster, neighbours, orient, send_faces, counts):
    device_total = N_GX * N_GY * N_GZ
    face_count = 4 * E_DEV
    element_total = device_total * E_DEV
    block_width = FACE_BASIS * QUANTITIES
    owner_device = jnp.arange(element_total, dtype=jnp.int32) // E_DEV
    coordinates = [owner_device // (N_GY * N_GZ), (owner_device // N_GZ) % N_GY, owner_device % N_GZ]
    axis_sizes = [N_GX, N_GY, N_GZ]
    is_ghost = neighbours >= face_count
    remainder = jnp.maximum(neighbours - face_count, 0)
    direction = remainder // SLOTS
    slot_index = remainder % SLOTS
    axis_id = direction // 2
    shift_sign = jnp.where(direction % 2 == 0, -1, 1).astype(jnp.int32)
    inside_mesh = jnp.ones(neighbours.shape, dtype=bool)
    moved = []
    for axis_number in range(3):
        placed = coordinates[axis_number][None, :] + jnp.where(axis_id == axis_number, shift_sign, 0)
        inside_mesh = inside_mesh & (placed >= 0) & (placed < axis_sizes[axis_number])
        moved.append(jnp.clip(placed, 0, axis_sizes[axis_number] - 1))
    sender = ((moved[0] * N_GY + moved[1]) * N_GZ + moved[2]).astype(jnp.int32)
    face_id = send_faces.reshape(-1)[direction * (device_total * SLOTS) + sender * SLOTS + slot_index]
    slot_alive = slot_index < counts.reshape(-1)[direction * device_total + sender]
    zero_column = device_total * face_count
    remote_index = jnp.where(inside_mesh & slot_alive, sender * face_count + face_id, zero_column)
    global_index = jnp.where(is_ghost, remote_index, owner_device[None, :] * face_count + neighbours).astype(jnp.int32)

    stiff_stack = derivative_stiffness.reshape(3 * BASIS, BASIS)
    volume_stack = volume_stiffness.reshape(3 * BASIS, BASIS)
    project_stack = face_project.reshape(4 * FACE_BASIS, BASIS)
    rotation_stack = face_rotation.reshape(3 * FACE_BASIS, FACE_BASIS)
    lift_join = face_lift.transpose(1, 0, 2).reshape(BASIS, 4 * FACE_BASIS)
    orient_picks = (orient.reshape(-1)[None, :] == jnp.arange(3, dtype=jnp.int32)[:, None]).astype(jnp.float32)

    own_total = jnp.zeros_like(solution)
    flux_total = jnp.zeros_like(solution)
    for substep in range(SUBSTEPS):
        weights, finish = time_weights(cluster, substep)
        derivatives = derivative_terms(solution, jacobians, stiff_stack)
        integral = weights[0][None, None, :] * derivatives[0]
        for power_index in range(1, DERIVATIVES):
            integral = integral + weights[power_index][None, None, :] * derivatives[power_index]
        projected = jnp.dot(project_stack, integral.reshape(BASIS, -1), precision=highest).reshape(4, FACE_BASIS, QUANTITIES, element_total)
        face_table = projected.reshape(4, block_width, device_total, E_DEV).transpose(1, 2, 0, 3).reshape(block_width, device_total * face_count)
        face_table = jnp.concatenate([face_table, jnp.zeros((block_width, 1), jnp.float32)], axis=1)
        gathered = jnp.take(face_table, global_index.reshape(-1), axis=1)
        rotated = jnp.dot(rotation_stack, gathered.reshape(FACE_BASIS, -1), precision=highest).reshape(3, FACE_BASIS, QUANTITIES, 4 * element_total)
        chosen = jnp.einsum("hfqx,hx->fqx", rotated, orient_picks, precision=highest).reshape(FACE_BASIS, QUANTITIES, 4, element_total)
        neighbour_part = jnp.einsum("fqie,iqpe->ifpe", chosen, neighbour_solver, precision=highest)
        local_part = jnp.einsum("ifqe,iqpe->ifpe", projected, local_solver, precision=highest)
        flux_step = jnp.dot(lift_join, (local_part + neighbour_part).reshape(4 * FACE_BASIS, -1), precision=highest).reshape(BASIS, QUANTITIES, element_total)
        own_total = own_total + integral
        flux_total = flux_total + flux_step
        updated = solution + volume_term(own_total, jacobians, volume_stack) - flux_total
        ending = finish[None, None, :]
        solution = jnp.where(ending, updated, solution)
        own_total = jnp.where(ending, 0.0, own_total)
        flux_total = jnp.where(ending, 0.0, flux_total)
    return solution
```

```python
import functools
import math

import jax
import jax.numpy as jnp
from jax import lax
from jax.experimental import pallas as pl
from jax.experimental.pallas import tpu as pltpu
from jax.sharding import PartitionSpec as P

DERIVATIVES = 6
SUBSTEPS = 4
SPAN = 1.0
F32 = jnp.float32
BF16 = jnp.bfloat16
AXES = ("gx", "gy", "gz")


def rounded(size, unit):
    return -(-size // unit) * unit


def halves(value):
    high = value.astype(BF16)
    return high, (value - high.astype(F32)).astype(BF16)


def product(left, right):
    return jnp.dot(left, right, preferred_element_type=F32)


def exchange_plan(mesh):
    plan = []
    for number, axis in enumerate(AXES):
        size = mesh.shape[axis]
        if size == 1:
            continue
        if size == 2:
            plan.append((number, size, "pair0"))
        elif size % 2 == 0:
            plan.append((number, size, "pair0"))
            plan.append((number, size, "pair1"))
        else:
            plan.append((number, size, "up"))
            plan.append((number, size, "down"))
    return tuple(plan)


def partners(size, kind):
    if kind == "up":
        return [(i, (i + 1) % size) for i in range(size)]
    if kind == "down":
        return [(i, (i - 1) % size) for i in range(size)]
    first = 0 if kind == "pair0" else 1
    pairs = []
    for i in range(first, size + first, 2):
        low, high = i % size, (i + 1) % size
        pairs += [(low, high), (high, low)]
    return pairs


def lists_of(entry):
    number, size, kind = entry
    place = lax.axis_index(AXES[number])
    if kind == "up":
        return 2 * number, 2 * number, place > 0
    if kind == "down":
        return 2 * number + 1, 2 * number + 1, place < size - 1
    parity = lax.rem(place, 2)
    upper = parity if kind == "pair0" else 1 - parity
    exists = jnp.where(upper == 1, place > 0, place < size - 1)
    return 2 * number + upper, 2 * number + 1 - upper, exists


class Sizes:
    def __init__(self, solution, face_project, send_faces, plan):
        self.basis, self.quantities, self.elements = solution.shape
        self.faces, self.face_basis, _ = face_project.shape
        self.slots = send_faces.shape[1]
        self.plan = plan
        self.padded = rounded(self.basis, 16)
        self.face_rows = rounded(self.face_basis, 8)
        self.block = self.quantities * self.face_rows
        self.block_padded = rounded(self.block, 16)
        self.columns = self.quantities * self.elements
        self.face_total = self.faces * self.elements
        self.lifted = self.faces * self.face_rows
        self.rotations = 3

    def groups(self):
        return [(k, min(16, self.basis - k)) for k in range(0, self.basis, 16)]


def left_parts(scratch, pieces, width):
    scratch[...] = jnp.zeros_like(scratch)
    for row, column, value in pieces:
        high = value.astype(BF16).astype(F32)
        rows, columns = value.shape
        scratch[row : row + rows, column : column + columns] = high
        scratch[row : row + rows, width + column : width + column + columns] = high
        scratch[row : row + rows, 2 * width + column : 2 * width + column + columns] = value - high
    return scratch[...].astype(BF16)


def one_hot(shape, targets, offset):
    rows = lax.broadcasted_iota(jnp.int32, shape, 0)
    return jnp.where(rows == targets - offset, 1.0, 0.0).astype(BF16)


def period_of(cluster):
    return jnp.left_shift(jnp.ones_like(cluster), cluster)


def weights_of(cluster, substep):
    offset = (substep & (period_of(cluster) - 1)).astype(F32)
    step = SPAN / SUBSTEPS
    upper, lower = (offset + 1.0) * step, offset * step
    rows, high, low = [], upper, lower
    for power in range(DERIVATIVES):
        rows.append((high - low) * (1.0 / math.factorial(power + 1)))
        high, low = high * upper, low * lower
    return rows


def put_halves(target, width, row, column, value):
    high, low = halves(value)
    rows, columns = value.shape
    target[row : row + rows, column : column + columns] = high
    target[width + row : width + row + rows, column : column + columns] = low
    target[2 * width + row : 2 * width + row + rows, column : column + columns] = high


def contract(z, mixed, jacobians, first, rows):
    totals = [None] * z.quantities
    for d in range(3):
        for q in range(z.quantities):
            start = d * z.basis + first
            value = mixed[start : start + rows, q * z.elements : (q + 1) * z.elements]
            for p in range(z.quantities):
                term = value * jacobians[q, p, d : d + 1, :]
                totals[p] = term if totals[p] is None else totals[p] + term
    return totals


def full_rows(value, rows):
    short = rows - value.shape[0]
    if short == 0:
        return value
    return jnp.concatenate([value, jnp.zeros((short, value.shape[1]), value.dtype)], axis=0)


def predict(z, substep, cluster, state, jacobians, stiff, project, send_hot, outgoing, table, faces, moments, rhs, mixed, total, weights):
    e = z.elements
    for power, row in enumerate(weights_of(cluster[...], substep)):
        weights[power] = jnp.broadcast_to(row, (8, e))
    for q in range(z.quantities):
        for first, rows in z.groups():
            value = state(q, first, rows)
            total[q, first : first + rows, :] = value * weights[0, 0:1, :]
            put_halves(rhs, z.padded, first, q * e, full_rows(value, 16))

    def derivative(power, carry):
        mixed[...] = product(stiff[...], rhs[...])
        weight = weights[power]
        for first, rows in z.groups():
            sums = contract(z, mixed, jacobians, first, rows)
            for p in range(z.quantities):
                total[p, first : first + rows, :] += sums[p] * weight[0:1, :]
                put_halves(rhs, z.padded, first, p * e, full_rows(sums[p], 16))
        return carry

    lax.fori_loop(1, DERIVATIVES, derivative, 0)
    for q in range(z.quantities):
        for first, rows in z.groups():
            put_halves(moments, z.padded, first, q * e, full_rows(total[q, first : first + rows, :], 16))
    projected = product(project[...], moments[...])
    faces[...] = projected
    r = z.face_rows
    for j in range(z.faces):
        pieces = [projected[j * r : (j + 1) * r, q * e : (q + 1) * e] for q in range(z.quantities)]
        high, low = halves(full_rows(jnp.concatenate(pieces, axis=0), z.block_padded))
        table[: z.block_padded, j * e : (j + 1) * e] = high
        table[z.block_padded :, j * e : (j + 1) * e] = low
    picked = product(table[...], send_hot[...])
    for t, target in enumerate(outgoing):
        columns = slice(t * z.slots, (t + 1) * z.slots)
        target[...] = picked[: z.block, columns] + picked[z.block_padded : z.block_padded + z.block, columns]


def first_kernel(z, *refs):
    count = len(z.plan)
    solution, jacobians, stiffness, projection, cluster, send_faces, counts = refs[:7]
    outgoing = refs[7 : 7 + count]
    table, faces, moments, stiff, project, send_hot = refs[7 + count : 13 + count]
    rhs, mixed, total, weights, wide_stiff, wide_project = refs[13 + count :]
    b = z.basis
    stiff[...] = left_parts(wide_stiff, [(d * b, 0, -stiffness[d]) for d in range(3)], z.padded)
    project[...] = left_parts(
        wide_project, [(j * z.face_rows, 0, projection[:, j, :]) for j in range(z.faces)], z.padded
    )
    slot = lax.broadcasted_iota(jnp.int32, (1, z.slots), 1)
    for t, entry in enumerate(z.plan):
        chosen = lists_of(entry)[0]
        wanted = jnp.where(slot < counts[0, chosen], send_faces[pl.ds(chosen, 1), :], -1)
        send_hot[:, t * z.slots : (t + 1) * z.slots] = one_hot((z.face_total, z.slots), wanted, 0)
    predict(
        z, 0, cluster, lambda q, k, n: solution[q, k : k + n, :], jacobians, stiff, project, send_hot,
        outgoing, table, faces, moments, rhs, mixed, total, weights,
    )


def tables_kernel(z, *refs):
    volume, lift, rotation, neighbours, orient = refs[:5]
    volume_left, lift_left, turned_left, picks, own_hot, far_hot = refs[5:11]
    wide_volume, wide_lift, wide_turned = refs[11:]
    e, r, f = z.elements, z.face_rows, z.face_basis
    volume_left[...] = left_parts(wide_volume, [(d * z.basis, 0, volume[d]) for d in range(3)], z.padded)
    plain, turned = [], []
    for i in range(z.faces):
        face = jnp.transpose(lift[:, i, :], (1, 0))
        plain.append((0, i * r, face))
        for o in range(z.rotations):
            value = jnp.dot(face, rotation[o], precision=lax.Precision.HIGHEST, preferred_element_type=F32)
            turned.append((0, o * z.lifted + i * r, value))
    lift_left[...] = left_parts(wide_lift, plain, z.lifted)
    turned_left[...] = left_parts(wide_turned, turned, z.rotations * z.lifted)
    for o in range(z.rotations):
        rows = [
            jnp.broadcast_to(jnp.where(orient[i : i + 1, :] == o, 1.0, 0.0), (r, e)) for i in range(z.faces)
        ]
        picks[o] = jnp.concatenate(rows, axis=0).astype(BF16)
    for i in range(z.faces):
        wanted = neighbours[i : i + 1, :]
        own_hot[:, i * e : (i + 1) * e] = one_hot((z.face_total, e), wanted, 0)
        for t, entry in enumerate(z.plan):
            _, direction, exists = lists_of(entry)
            offset = jnp.where(exists, z.face_total + direction * z.slots, -z.slots)
            far_hot[t * z.slots : (t + 1) * z.slots, i * e : (i + 1) * e] = one_hot((z.slots, e), wanted, offset)


def inner_kernel(z, running, table, faces, moments, jacobians, local_solver, volume_left, lift_left, own_hot, gathered, partial, mixed, rhs):
    e, r = z.elements, z.face_rows
    picked = product(table[...], own_hot[...])
    gathered[...] = picked[: z.block, :] + picked[z.block_padded : z.block_padded + z.block, :]
    for i in range(z.faces):
        sums = [None] * z.quantities
        for q in range(z.quantities):
            value = faces[i * r : (i + 1) * r, q * e : (q + 1) * e]
            for p in range(z.quantities):
                term = value * local_solver[q, p, i : i + 1, :]
                sums[p] = term if sums[p] is None else sums[p] + term
        for p in range(z.quantities):
            partial_rows = slice(i * r, (i + 1) * r)
            mixed[partial_rows, p * e : (p + 1) * e] = sums[p]
    put_halves(rhs, z.lifted, 0, 0, mixed[: z.lifted, :])
    lifted = product(lift_left[...], rhs[...])
    for q in range(z.quantities):
        partial[q] = running[q] - lifted[:, q * e : (q + 1) * e]
    mixed[...] = product(volume_left[...], moments[...])
    for first, rows in z.groups():
        sums = contract(z, mixed, jacobians, first, rows)
        for p in range(z.quantities):
            partial[p, first : first + rows, :] += sums[p]


def neighbour_flux(z, incoming, gathered, neighbour_solver, picks, far_hot, turned_left, received, blocks, turned):
    e, r, b = z.elements, z.face_rows, z.block
    for t, source in enumerate(incoming):
        high, low = halves(full_rows(source[...], z.block_padded))
        received[: z.block_padded, t * z.slots : (t + 1) * z.slots] = high
        received[z.block_padded :, t * z.slots : (t + 1) * z.slots] = low
    picked = product(received[...], far_hot[...])
    blocks[...] = gathered[...] + picked[:b, :] + picked[z.block_padded : z.block_padded + b, :]
    width = z.rotations * z.lifted
    for i in range(0, z.faces, 2):
        per_face = []
        for j in (i, i + 1):
            sums = [None] * z.quantities
            for q in range(z.quantities):
                value = blocks[q * r : (q + 1) * r, j * e : (j + 1) * e]
                for p in range(z.quantities):
                    term = value * neighbour_solver[q, p, j : j + 1, :]
                    sums[p] = term if sums[p] is None else sums[p] + term
            per_face.append(sums)
        for p in range(z.quantities):
            high, low = halves(jnp.concatenate([per_face[0][p], per_face[1][p]], axis=0))
            for o in range(z.rotations):
                pick = picks[o, i * r : (i + 2) * r, :]
                row = o * z.lifted + i * r
                chosen = high * pick
                turned[row : row + 2 * r, p * e : (p + 1) * e] = chosen
                turned[2 * width + row : 2 * width + row + 2 * r, p * e : (p + 1) * e] = chosen
                turned[width + row : width + row + 2 * r, p * e : (p + 1) * e] = low * pick
    return product(turned_left[...], turned[...])


def outer_kernel(z, substep, *refs):
    count = len(z.plan)
    incoming = refs[:count]
    (gathered, partial, solution, neighbour_solver, picks, far_hot, turned_left, jacobians, stiff, project, send_hot, cluster) = refs[
        count : count + 12
    ]
    outgoing = refs[count + 12 : 2 * count + 12]
    table, faces, moments, updated, running = refs[2 * count + 12 : 2 * count + 17]
    rhs, mixed, total, weights, received, blocks, turned = refs[2 * count + 17 :]
    e = z.elements
    flux = neighbour_flux(
        z, incoming, gathered, neighbour_solver, picks, far_hot, turned_left, received, blocks, turned
    )
    ending = ((substep + 1) & (period_of(cluster[...]) - 1)) == 0
    for q in range(z.quantities):
        value = partial[q] - flux[:, q * e : (q + 1) * e]
        running[q] = value
        updated[q] = jnp.where(ending, value, solution[q])
    predict(
        z, substep + 1, cluster, lambda q, k, n: updated[q, k : k + n, :], jacobians, stiff, project, send_hot,
        outgoing, table, faces, moments, rhs, mixed, total, weights,
    )


def last_kernel(z, *refs):
    count = len(z.plan)
    incoming = refs[:count]
    gathered, partial, neighbour_solver, picks, far_hot, turned_left = refs[count : count + 6]
    advanced = refs[count + 6]
    received, blocks, turned = refs[count + 7 :]
    e = z.elements
    flux = neighbour_flux(
        z, incoming, gathered, neighbour_solver, picks, far_hot, turned_left, received, blocks, turned
    )
    for q in range(z.quantities):
        advanced[q] = partial[q] - flux[:, q * e : (q + 1) * e]


def call(body, outs, scratch, cost, arguments, scalars=()):
    in_specs = [
        pl.BlockSpec(memory_space=pltpu.SMEM if n in scalars else pltpu.VMEM) for n in range(len(arguments))
    ]
    return pl.pallas_call(
        body,
        out_shape=[jax.ShapeDtypeStruct(shape, kind) for shape, kind in outs],
        in_specs=in_specs,
        out_specs=[pl.BlockSpec(memory_space=pltpu.VMEM)] * len(outs),
        scratch_shapes=[pltpu.VMEM(shape, kind) for shape, kind in scratch],
        cost_estimate=pl.CostEstimate(flops=cost, bytes_accessed=1 << 20, transcendentals=0),
        compiler_params=pltpu.CompilerParams(vmem_limit_bytes=24 << 20),
    )(*arguments)


def local(
    plan,
    solution,
    jacobians,
    derivative_stiffness,
    volume_stiffness,
    face_project,
    face_lift,
    face_rotation,
    local_solver,
    neighbour_solver,
    cluster,
    neighbours,
    orient,
    send_faces,
    counts,
):
    z = Sizes(solution, face_project, send_faces, plan)
    count = len(plan)
    state = solution.transpose(1, 0, 2)
    jacobians = jacobians.transpose(1, 2, 0, 3)
    local_solver = local_solver.transpose(1, 2, 0, 3)
    neighbour_solver = neighbour_solver.transpose(1, 2, 0, 3)
    projection = face_project.transpose(1, 0, 2)
    lift = face_lift.transpose(2, 0, 1)
    cluster = cluster.reshape(1, -1)
    counts = counts.reshape(1, -1)

    block = ((z.block, z.slots), F32)
    table = ((2 * z.block_padded, z.face_total), BF16)
    faces = ((z.lifted, z.columns), F32)
    moments = ((3 * z.padded, z.columns), BF16)
    stiff = ((3 * z.basis, 3 * z.padded), BF16)
    project = ((z.lifted, 3 * z.padded), BF16)
    field = ((z.quantities, z.basis, z.elements), F32)
    gathered = ((z.block, z.face_total), F32)
    send_hot = ((z.face_total, count * z.slots), BF16)
    far_hot = ((count * z.slots, z.face_total), BF16)
    own_hot = ((z.face_total, z.face_total), BF16)
    lift_left = ((z.basis, 3 * z.lifted), BF16)
    turned_left = ((z.basis, 3 * z.rotations * z.lifted), BF16)
    picks = ((z.rotations, z.lifted, z.elements), BF16)
    mixed = ((3 * z.basis, z.columns), F32)
    weights = ((DERIVATIVES, 8, z.elements), F32)
    received = ((2 * z.block_padded, count * z.slots), BF16)
    turned = ((3 * z.rotations * z.lifted, z.columns), BF16)

    def wide(entry):
        return (entry[0], F32)

    def trade(outgoing):
        return [
            lax.ppermute(value, AXES[number], partners(size, kind))
            for value, (number, size, kind) in zip(outgoing, plan)
        ]

    results = call(
        functools.partial(first_kernel, z),
        [block] * count + [table, faces, moments, stiff, project, send_hot],
        [moments, mixed, field, weights, wide(stiff), wide(project)],
        10_000_000,
        (state, jacobians, derivative_stiffness, projection, cluster, send_faces, counts),
        scalars=(6,),
    )
    outgoing = results[:count]
    table_now, faces_now, moments_now, stiff_left, project_left, send_matrix = results[count:]
    running = state
    for substep in range(SUBSTEPS):
        incoming = trade(outgoing)
        if substep == 0:
            volume_left, lift_plain, lift_turned, orient_picks, own_matrix, far_matrix = call(
                functools.partial(tables_kernel, z),
                [stiff, lift_left, turned_left, picks, own_hot, far_hot],
                [wide(stiff), wide(lift_left), wide(turned_left)],
                1_000_000,
                (volume_stiffness, lift, face_rotation, neighbours, orient),
            )
        gathered_now, partial = call(
            functools.partial(inner_kernel, z),
            [gathered, field],
            [mixed, ((3 * z.lifted, z.columns), BF16)],
            10_000_000,
            (running, table_now, faces_now, moments_now, jacobians, local_solver, volume_left, lift_plain, own_matrix),
        )
        if substep == SUBSTEPS - 1:
            (advanced,) = call(
                functools.partial(last_kernel, z),
                [field],
                [received, gathered, turned],
                10_000_000,
                (*incoming, gathered_now, partial, neighbour_solver, orient_picks, far_matrix, lift_turned),
            )
            return advanced.transpose(1, 0, 2)
        results = call(
            functools.partial(outer_kernel, z, substep),
            [block] * count + [table, faces, moments, field, field],
            [moments, mixed, field, weights, received, gathered, turned],
            10_000_000,
            (
                *incoming, gathered_now, partial, state, neighbour_solver, orient_picks, far_matrix, lift_turned,
                jacobians, stiff_left, project_left, send_matrix, cluster,
            ),
        )
        outgoing = results[:count]
        table_now, faces_now, moments_now, state, running = results[count:]


def solution(mesh):
    spread = ("gx", "gy", "gz")
    return jax.shard_map(
        functools.partial(local, exchange_plan(mesh)),
        mesh=mesh,
        in_specs=(
            P(None, None, spread),
            P(None, None, None, spread),
            P(),
            P(),
            P(),
            P(),
            P(),
            P(None, None, None, spread),
            P(None, None, None, spread),
            P(spread),
            P(None, spread),
            P(None, spread),
            P(None, spread),
            P(None, spread),
        ),
        out_specs=P(None, None, spread),
        check_vma=False,
    )
```

```python
import functools
import math

import jax
import jax.numpy as jnp
from jax import lax
from jax.experimental import pallas as pl
from jax.experimental.pallas import tpu as pltpu
from jax.sharding import PartitionSpec as P

DERIVATIVES = 6
SUBSTEPS = 4
SPAN = 1.0
F32 = jnp.float32
BF16 = jnp.bfloat16
AXES = ("gx", "gy", "gz")


def rounded(size, unit):
    return -(-size // unit) * unit


def halves(value):
    high = value.astype(BF16)
    return high, (value - high.astype(F32)).astype(BF16)


def product(left, right):
    return jnp.dot(left, right, preferred_element_type=F32)


def exchange_plan(mesh):
    plan = []
    for number, axis in enumerate(AXES):
        size = mesh.shape[axis]
        if size == 1:
            continue
        if size == 2:
            plan.append((number, size, "pair0"))
        elif size % 2 == 0:
            plan.append((number, size, "pair0"))
            plan.append((number, size, "pair1"))
        else:
            plan.append((number, size, "up"))
            plan.append((number, size, "down"))
    return tuple(plan)


def partners(sizes, entry):
    number, size, kind = entry
    spare = [other for other in (2, 0, 1) if other != number and sizes[other] % 2 == 0]
    pairs = []
    for flat in range(math.prod(sizes)):
        place = [flat // (sizes[1] * sizes[2]), flat // sizes[2] % sizes[1], flat % sizes[2]]
        source = flat
        here = place[number]
        if kind in ("up", "down"):
            place[number] = (here + (1 if kind == "up" else -1)) % size
        elif kind == "pair0":
            place[number] = here ^ 1
        elif 0 < here < size - 1:
            place[number] = ((here + 1) ^ 1) - 1
        elif spare:
            place[spare[0]] ^= 1
        else:
            place[number] = size - 1 - here
        pairs.append((source, (place[0] * sizes[1] + place[1]) * sizes[2] + place[2]))
    return pairs


def lists_of(entry):
    number, size, kind = entry
    place = lax.axis_index(AXES[number])
    if kind == "up":
        return 2 * number, 2 * number, place > 0
    if kind == "down":
        return 2 * number + 1, 2 * number + 1, place < size - 1
    parity = lax.rem(place, 2)
    upper = parity if kind == "pair0" else 1 - parity
    exists = jnp.where(upper == 1, place > 0, place < size - 1)
    return 2 * number + upper, 2 * number + 1 - upper, exists


class Sizes:
    def __init__(self, solution, face_project, send_faces, plan):
        self.basis, self.quantities, self.elements = solution.shape
        self.faces, self.face_basis, _ = face_project.shape
        self.slots = send_faces.shape[1]
        self.plan = plan
        self.padded = rounded(self.basis, 16)
        self.face_rows = rounded(self.face_basis, 8)
        self.block = self.quantities * self.face_rows
        self.block_padded = rounded(self.block, 16)
        self.columns = self.quantities * self.elements
        self.face_total = self.faces * self.elements
        self.lifted = self.faces * self.face_rows
        self.rotations = 3

    def groups(self):
        return [(k, min(16, self.basis - k)) for k in range(0, self.basis, 16)]


def left_parts(scratch, pieces, width):
    scratch[...] = jnp.zeros_like(scratch)
    for row, column, value in pieces:
        high = value.astype(BF16).astype(F32)
        rows, columns = value.shape
        scratch[row : row + rows, column : column + columns] = high
        scratch[row : row + rows, width + column : width + column + columns] = high
        scratch[row : row + rows, 2 * width + column : 2 * width + column + columns] = value - high
    return scratch[...].astype(BF16)


def one_hot(shape, targets, offset):
    rows = lax.broadcasted_iota(jnp.int32, shape, 0)
    return jnp.where(rows == targets - offset, 1.0, 0.0).astype(BF16)


def period_of(cluster):
    return jnp.left_shift(jnp.ones_like(cluster), cluster)


def weights_of(cluster, substep):
    offset = (substep & (period_of(cluster) - 1)).astype(F32)
    step = SPAN / SUBSTEPS
    upper, lower = (offset + 1.0) * step, offset * step
    rows, high, low = [], upper, lower
    for power in range(DERIVATIVES):
        rows.append((high - low) * (1.0 / math.factorial(power + 1)))
        high, low = high * upper, low * lower
    return rows


def put_halves(target, width, row, column, value):
    high, low = halves(value)
    rows, columns = value.shape
    target[row : row + rows, column : column + columns] = high
    target[width + row : width + row + rows, column : column + columns] = low
    target[2 * width + row : 2 * width + row + rows, column : column + columns] = high


def contract(z, mixed, jacobians, first, rows):
    totals = [None] * z.quantities
    for q in range(z.quantities):
        for d in range(3):
            start = d * z.basis + first
            value = mixed[start : start + rows, q * z.elements : (q + 1) * z.elements]
            for p in range(z.quantities):
                term = value * jacobians[q, p, d : d + 1, :]
                totals[p] = term if totals[p] is None else totals[p] + term
    return totals


def full_rows(value, rows):
    short = rows - value.shape[0]
    if short == 0:
        return value
    return jnp.concatenate([value, jnp.zeros((short, value.shape[1]), value.dtype)], axis=0)


def predict(z, substep, cluster, state, jacobians, stiff, project, send_hot, outgoing, table, faces, moments, rhs, mixed, total, weights):
    e = z.elements
    for power, row in enumerate(weights_of(cluster[...], substep)):
        weights[power] = jnp.broadcast_to(row, (8, e))
    for q in range(z.quantities):
        for first, rows in z.groups():
            value = state(q, first, rows)
            total[q, first : first + rows, :] = value * weights[0, 0:1, :]
            put_halves(rhs, z.padded, first, q * e, full_rows(value, 16))

    def derivative(power, carry):
        mixed[...] = product(stiff[...], rhs[...])
        weight = weights[power]
        for first, rows in z.groups():
            sums = contract(z, mixed, jacobians, first, rows)
            for p in range(z.quantities):
                total[p, first : first + rows, :] += sums[p] * weight[0:1, :]
                put_halves(rhs, z.padded, first, p * e, full_rows(sums[p], 16))
        return carry

    lax.fori_loop(1, DERIVATIVES, derivative, 0)
    for q in range(z.quantities):
        for first, rows in z.groups():
            put_halves(moments, z.padded, first, q * e, full_rows(total[q, first : first + rows, :], 16))
    projected = product(project[...], moments[...])
    faces[...] = projected
    r = z.face_rows
    for j in range(z.faces):
        pieces = [projected[j * r : (j + 1) * r, q * e : (q + 1) * e] for q in range(z.quantities)]
        high, low = halves(full_rows(jnp.concatenate(pieces, axis=0), z.block_padded))
        table[: z.block_padded, j * e : (j + 1) * e] = high
        table[z.block_padded :, j * e : (j + 1) * e] = low
    picked = product(table[...], send_hot[...])
    for t, target in enumerate(outgoing):
        columns = slice(t * z.slots, (t + 1) * z.slots)
        target[...] = picked[: z.block, columns] + picked[z.block_padded : z.block_padded + z.block, columns]


def first_kernel(z, *refs):
    count = len(z.plan)
    outgoing = refs[7 : 7 + count]
    table, faces, moments, stiff, project, send_hot = refs[7 + count : 13 + count]
    rhs, mixed, total, weights, wide_stiff, wide_project = refs[13 + count : 19 + count]
    held, arrived = refs[19 + count : 26 + count], refs[26 + count]
    copies = [pltpu.make_async_copy(refs[n], held[n], arrived.at[n]) for n in range(7)]
    for n in (5, 6, 2, 3, 4, 0, 1):
        copies[n].start()
    solution, jacobians, stiffness, projection, cluster, send_faces, counts = held
    b = z.basis
    for n in (5, 6):
        copies[n].wait()
    slot = lax.broadcasted_iota(jnp.int32, (1, z.slots), 1)
    for t, entry in enumerate(z.plan):
        chosen = lists_of(entry)[0]
        wanted = jnp.where(slot < counts[0, chosen], send_faces[pl.ds(chosen, 1), :], -1)
        send_hot[:, t * z.slots : (t + 1) * z.slots] = one_hot((z.face_total, z.slots), wanted, 0)
    for n in (2, 3, 4):
        copies[n].wait()
    stiff[...] = left_parts(wide_stiff, [(d * b, 0, -stiffness[d]) for d in range(3)], z.padded)
    project[...] = left_parts(
        wide_project, [(j * z.face_rows, 0, projection[:, j, :]) for j in range(z.faces)], z.padded
    )
    for n in (0, 1):
        copies[n].wait()
    predict(
        z, 0, cluster, lambda q, k, n: solution[q, k : k + n, :], jacobians, stiff, project, send_hot,
        outgoing, table, faces, moments, rhs, mixed, total, weights,
    )


def tables_kernel(z, *refs):
    volume, lift, rotation, neighbours, orient = refs[:5]
    volume_left, lift_left, turned_left, picks, own_hot, far_hot = refs[5:11]
    wide_volume, wide_lift, wide_turned = refs[11:]
    e, r, f = z.elements, z.face_rows, z.face_basis
    volume_left[...] = left_parts(wide_volume, [(d * z.basis, 0, volume[d]) for d in range(3)], z.padded)
    plain, turned = [], []
    for i in range(z.faces):
        face = jnp.transpose(lift[:, i, :], (1, 0))
        plain.append((0, i * r, face))
        for o in range(z.rotations):
            value = jnp.dot(face, rotation[o], precision=lax.Precision.HIGHEST, preferred_element_type=F32)
            turned.append((0, o * z.lifted + i * r, value))
    lift_left[...] = left_parts(wide_lift, plain, z.lifted)
    turned_left[...] = left_parts(wide_turned, turned, z.rotations * z.lifted)
    for o in range(z.rotations):
        rows = [
            jnp.broadcast_to(jnp.where(orient[i : i + 1, :] == o, 1.0, 0.0), (r, e)) for i in range(z.faces)
        ]
        picks[o] = jnp.concatenate(rows, axis=0).astype(BF16)
    for i in range(z.faces):
        wanted = neighbours[i : i + 1, :]
        own_hot[:, i * e : (i + 1) * e] = one_hot((z.face_total, e), wanted, 0)
        for t, entry in enumerate(z.plan):
            _, direction, exists = lists_of(entry)
            offset = jnp.where(exists, z.face_total + direction * z.slots, -z.slots)
            far_hot[t * z.slots : (t + 1) * z.slots, i * e : (i + 1) * e] = one_hot((z.slots, e), wanted, offset)


def inner_kernel(z, running, table, faces, moments, jacobians, local_solver, volume_left, lift_left, own_hot, gathered, partial, mixed, rhs):
    e, r = z.elements, z.face_rows
    picked = product(table[...], own_hot[...])
    gathered[...] = picked[: z.block, :] + picked[z.block_padded : z.block_padded + z.block, :]
    for i in range(z.faces):
        sums = [None] * z.quantities
        for q in range(z.quantities):
            value = faces[i * r : (i + 1) * r, q * e : (q + 1) * e]
            for p in range(z.quantities):
                term = value * local_solver[q, p, i : i + 1, :]
                sums[p] = term if sums[p] is None else sums[p] + term
        for p in range(z.quantities):
            partial_rows = slice(i * r, (i + 1) * r)
            mixed[partial_rows, p * e : (p + 1) * e] = sums[p]
    put_halves(rhs, z.lifted, 0, 0, mixed[: z.lifted, :])
    lifted = product(lift_left[...], rhs[...])
    for q in range(z.quantities):
        partial[q] = running[q] - lifted[:, q * e : (q + 1) * e]
    mixed[...] = product(volume_left[...], moments[...])
    for first, rows in z.groups():
        sums = contract(z, mixed, jacobians, first, rows)
        for p in range(z.quantities):
            partial[p, first : first + rows, :] += sums[p]


def neighbour_flux(z, incoming, gathered, neighbour_solver, picks, far_hot, turned_left, received, blocks, turned):
    e, r, b = z.elements, z.face_rows, z.block
    for t, source in enumerate(incoming):
        high, low = halves(full_rows(source[...], z.block_padded))
        received[: z.block_padded, t * z.slots : (t + 1) * z.slots] = high
        received[z.block_padded :, t * z.slots : (t + 1) * z.slots] = low
    picked = product(received[...], far_hot[...])
    blocks[...] = gathered[...] + picked[:b, :] + picked[z.block_padded : z.block_padded + b, :]
    width = z.rotations * z.lifted
    for i in range(0, z.faces, 2):
        per_face = []
        for j in (i, i + 1):
            sums = [None] * z.quantities
            for q in range(z.quantities):
                value = blocks[q * r : (q + 1) * r, j * e : (j + 1) * e]
                for p in range(z.quantities):
                    term = value * neighbour_solver[q, p, j : j + 1, :]
                    sums[p] = term if sums[p] is None else sums[p] + term
            per_face.append(sums)
        for p in range(z.quantities):
            high, low = halves(jnp.concatenate([per_face[0][p], per_face[1][p]], axis=0))
            for o in range(z.rotations):
                pick = picks[o, i * r : (i + 2) * r, :]
                row = o * z.lifted + i * r
                chosen = high * pick
                turned[row : row + 2 * r, p * e : (p + 1) * e] = chosen
                turned[2 * width + row : 2 * width + row + 2 * r, p * e : (p + 1) * e] = chosen
                turned[width + row : width + row + 2 * r, p * e : (p + 1) * e] = low * pick
    return product(turned_left[...], turned[...])


def outer_kernel(z, substep, *refs):
    count = len(z.plan)
    incoming = refs[:count]
    (gathered, partial, solution, neighbour_solver, picks, far_hot, turned_left, jacobians, stiff, project, send_hot, cluster) = refs[
        count : count + 12
    ]
    outgoing = refs[count + 12 : 2 * count + 12]
    table, faces, moments, updated, running = refs[2 * count + 12 : 2 * count + 17]
    rhs, mixed, total, weights, received, blocks, turned = refs[2 * count + 17 :]
    e = z.elements
    flux = neighbour_flux(
        z, incoming, gathered, neighbour_solver, picks, far_hot, turned_left, received, blocks, turned
    )
    ending = ((substep + 1) & (period_of(cluster[...]) - 1)) == 0
    for q in range(z.quantities):
        value = partial[q] - flux[:, q * e : (q + 1) * e]
        running[q] = value
        updated[q] = jnp.where(ending, value, solution[q])
    predict(
        z, substep + 1, cluster, lambda q, k, n: updated[q, k : k + n, :], jacobians, stiff, project, send_hot,
        outgoing, table, faces, moments, rhs, mixed, total, weights,
    )


def last_kernel(z, *refs):
    count = len(z.plan)
    incoming = refs[:count]
    gathered, partial, neighbour_solver, picks, far_hot, turned_left = refs[count : count + 6]
    advanced = refs[count + 6]
    received, blocks, turned = refs[count + 7 :]
    e = z.elements
    flux = neighbour_flux(
        z, incoming, gathered, neighbour_solver, picks, far_hot, turned_left, received, blocks, turned
    )
    for q in range(z.quantities):
        advanced[q] = partial[q] - flux[:, q * e : (q + 1) * e]


def call(body, outs, scratch, cost, arguments, space=pltpu.VMEM, more=()):
    in_specs = [pl.BlockSpec(memory_space=space)] * len(arguments)
    return pl.pallas_call(
        body,
        out_shape=[jax.ShapeDtypeStruct(shape, kind) for shape, kind in outs],
        in_specs=in_specs,
        out_specs=[pl.BlockSpec(memory_space=pltpu.VMEM)] * len(outs),
        scratch_shapes=[*(pltpu.VMEM(shape, kind) for shape, kind in scratch), *more],
        cost_estimate=pl.CostEstimate(flops=cost, bytes_accessed=1 << 20, transcendentals=0),
        compiler_params=pltpu.CompilerParams(vmem_limit_bytes=24 << 20),
    )(*arguments)


def local(
    plan,
    solution,
    jacobians,
    derivative_stiffness,
    volume_stiffness,
    face_project,
    face_lift,
    face_rotation,
    local_solver,
    neighbour_solver,
    cluster,
    neighbours,
    orient,
    send_faces,
    counts,
):
    z = Sizes(solution, face_project, send_faces, plan)
    count = len(plan)
    sizes = [lax.axis_size(axis) for axis in AXES]
    state = solution.transpose(1, 0, 2)
    jacobians = jacobians.transpose(1, 2, 0, 3)
    local_solver = local_solver.transpose(1, 2, 0, 3)
    neighbour_solver = neighbour_solver.transpose(1, 2, 0, 3)
    projection = face_project.transpose(1, 0, 2)
    lift = face_lift.transpose(2, 0, 1)
    cluster = cluster.reshape(1, -1)
    counts = counts.reshape(1, -1)

    block = ((z.block, z.slots), F32)
    table = ((2 * z.block_padded, z.face_total), BF16)
    faces = ((z.lifted, z.columns), F32)
    moments = ((3 * z.padded, z.columns), BF16)
    stiff = ((3 * z.basis, 3 * z.padded), BF16)
    project = ((z.lifted, 3 * z.padded), BF16)
    field = ((z.quantities, z.basis, z.elements), F32)
    gathered = ((z.block, z.face_total), F32)
    send_hot = ((z.face_total, count * z.slots), BF16)
    far_hot = ((count * z.slots, z.face_total), BF16)
    own_hot = ((z.face_total, z.face_total), BF16)
    lift_left = ((z.basis, 3 * z.lifted), BF16)
    turned_left = ((z.basis, 3 * z.rotations * z.lifted), BF16)
    picks = ((z.rotations, z.lifted, z.elements), BF16)
    mixed = ((3 * z.basis, z.columns), F32)
    weights = ((DERIVATIVES, 8, z.elements), F32)
    received = ((2 * z.block_padded, count * z.slots), BF16)
    turned = ((3 * z.rotations * z.lifted, z.columns), BF16)

    def wide(entry):
        return (entry[0], F32)

    def trade(outgoing):
        return [
            lax.ppermute(value, AXES, partners(sizes, entry)) for value, entry in zip(outgoing, plan)
        ]

    first_arguments = (state, jacobians, derivative_stiffness, projection, cluster, send_faces, counts)
    results = call(
        functools.partial(first_kernel, z),
        [block] * count + [table, faces, moments, stiff, project, send_hot],
        [moments, mixed, field, weights, wide(stiff), wide(project)],
        10_000_000,
        first_arguments,
        space=pltpu.HBM,
        more=[
            *(pltpu.VMEM(value.shape, value.dtype) for value in first_arguments[:-1]),
            pltpu.SMEM(counts.shape, counts.dtype),
            pltpu.SemaphoreType.DMA((len(first_arguments),)),
        ],
    )
    outgoing = results[:count]
    table_now, faces_now, moments_now, stiff_left, project_left, send_matrix = results[count:]
    running = state
    for substep in range(SUBSTEPS):
        incoming = trade(outgoing)
        if substep == 0:
            volume_left, lift_plain, lift_turned, orient_picks, own_matrix, far_matrix = call(
                functools.partial(tables_kernel, z),
                [stiff, lift_left, turned_left, picks, own_hot, far_hot],
                [wide(stiff), wide(lift_left), wide(turned_left)],
                1_000_000,
                (volume_stiffness, lift, face_rotation, neighbours, orient),
            )
        gathered_now, partial = call(
            functools.partial(inner_kernel, z),
            [gathered, field],
            [mixed, ((3 * z.lifted, z.columns), BF16)],
            10_000_000,
            (running, table_now, faces_now, moments_now, jacobians, local_solver, volume_left, lift_plain, own_matrix),
        )
        if substep == SUBSTEPS - 1:
            (advanced,) = call(
                functools.partial(last_kernel, z),
                [field],
                [received, gathered, turned],
                10_000_000,
                (*incoming, gathered_now, partial, neighbour_solver, orient_picks, far_matrix, lift_turned),
            )
            return advanced.transpose(1, 0, 2)
        results = call(
            functools.partial(outer_kernel, z, substep),
            [block] * count + [table, faces, moments, field, field],
            [moments, mixed, field, weights, received, gathered, turned],
            10_000_000,
            (
                *incoming, gathered_now, partial, state, neighbour_solver, orient_picks, far_matrix, lift_turned,
                jacobians, stiff_left, project_left, send_matrix, cluster,
            ),
        )
        outgoing = results[:count]
        table_now, faces_now, moments_now, state, running = results[count:]


def solution(mesh):
    spread = ("gx", "gy", "gz")
    return jax.shard_map(
        functools.partial(local, exchange_plan(mesh)),
        mesh=mesh,
        in_specs=(
            P(None, None, spread),
            P(None, None, None, spread),
            P(),
            P(),
            P(),
            P(),
            P(),
            P(None, None, None, spread),
            P(None, None, None, spread),
            P(spread),
            P(None, spread),
            P(None, spread),
            P(None, spread),
            P(None, spread),
        ),
        out_specs=P(None, None, spread),
        check_vma=False,
    )
```

```python
import functools
import math

import jax
import jax.numpy as jnp
from jax import lax
from jax.experimental import pallas as pl
from jax.experimental.pallas import tpu as pltpu
from jax.sharding import PartitionSpec as P

DERIVATIVES = 6
SUBSTEPS = 4
SPAN = 1.0
F32 = jnp.float32
BF16 = jnp.bfloat16
AXES = ("gx", "gy", "gz")


def rounded(size, unit):
    return -(-size // unit) * unit


def halves(value):
    high = value.astype(BF16)
    return high, (value - high.astype(F32)).astype(BF16)


def product(left, right):
    return jnp.dot(left, right, preferred_element_type=F32)


def exchange_plan(mesh):
    plan = []
    for number, axis in enumerate(AXES):
        size = mesh.shape[axis]
        if size == 1:
            continue
        if size == 2:
            plan.append((number, size, "pair0"))
        elif size % 2 == 0:
            plan.append((number, size, "pair0"))
            plan.append((number, size, "pair1"))
        else:
            plan.append((number, size, "up"))
            plan.append((number, size, "down"))
    return tuple(plan)


def partners(sizes, entry):
    number, size, kind = entry
    spare = [other for other in (2, 0, 1) if other != number and sizes[other] % 2 == 0]
    pairs = []
    for flat in range(math.prod(sizes)):
        place = [flat // (sizes[1] * sizes[2]), flat // sizes[2] % sizes[1], flat % sizes[2]]
        source = flat
        here = place[number]
        if kind in ("up", "down"):
            place[number] = (here + (1 if kind == "up" else -1)) % size
        elif kind == "pair0":
            place[number] = here ^ 1
        elif 0 < here < size - 1:
            place[number] = ((here + 1) ^ 1) - 1
        elif spare:
            place[spare[0]] ^= 1
        else:
            place[number] = size - 1 - here
        pairs.append((source, (place[0] * sizes[1] + place[1]) * sizes[2] + place[2]))
    return pairs


def lists_of(entry):
    number, size, kind = entry
    place = lax.axis_index(AXES[number])
    if kind == "up":
        return 2 * number, 2 * number, place > 0
    if kind == "down":
        return 2 * number + 1, 2 * number + 1, place < size - 1
    parity = lax.rem(place, 2)
    upper = parity if kind == "pair0" else 1 - parity
    exists = jnp.where(upper == 1, place > 0, place < size - 1)
    return 2 * number + upper, 2 * number + 1 - upper, exists


class Sizes:
    def __init__(self, solution, face_project, send_faces, plan):
        self.basis, self.quantities, self.elements = solution.shape
        self.faces, self.face_basis, _ = face_project.shape
        self.slots = send_faces.shape[1]
        self.plan = plan
        self.padded = rounded(self.basis, 16)
        self.face_rows = rounded(self.face_basis, 8)
        self.block = self.quantities * self.face_rows
        self.block_padded = rounded(self.block, 16)
        self.columns = self.quantities * self.elements
        self.face_total = self.faces * self.elements
        self.lifted = self.faces * self.face_rows
        self.rotations = 3

    def groups(self):
        return [(k, min(16, self.basis - k)) for k in range(0, self.basis, 16)]


def left_parts(scratch, pieces, width):
    scratch[...] = jnp.zeros_like(scratch)
    for row, column, value in pieces:
        high = value.astype(BF16).astype(F32)
        rows, columns = value.shape
        scratch[row : row + rows, column : column + columns] = high
        scratch[row : row + rows, width + column : width + column + columns] = high
        scratch[row : row + rows, 2 * width + column : 2 * width + column + columns] = value - high
    return scratch[...].astype(BF16)


def one_hot(shape, targets, offset):
    rows = lax.broadcasted_iota(jnp.int32, shape, 0)
    return jnp.where(rows == targets - offset, 1.0, 0.0).astype(BF16)


def period_of(cluster):
    return jnp.left_shift(jnp.ones_like(cluster), cluster)


def weights_of(cluster, substep):
    offset = (substep & (period_of(cluster) - 1)).astype(F32)
    step = SPAN / SUBSTEPS
    upper, lower = (offset + 1.0) * step, offset * step
    rows, high, low = [], upper, lower
    for power in range(DERIVATIVES):
        rows.append((high - low) * (1.0 / math.factorial(power + 1)))
        high, low = high * upper, low * lower
    return rows


def put_halves(target, width, row, column, value):
    high, low = halves(value)
    rows, columns = value.shape
    for part, piece in enumerate((high, low, high)):
        start = part * width + row
        if not isinstance(row, int):
            start = pl.multiple_of(start, 16)
        target[pl.ds(start, rows), pl.ds(column, columns)] = piece


def by_groups(z, group):
    whole = z.basis // 16
    group(0, 16)

    def later(index, carry):
        group(pl.multiple_of(index * 16, 16), 16)
        return carry

    lax.fori_loop(1, whole, later, 0)
    if z.basis % 16:
        group(whole * 16, z.basis % 16)


def contract(z, mixed, jacobians, first, rows):
    totals = [None] * z.quantities
    for q in range(z.quantities):
        for d in range(3):
            start = d * z.basis + first
            value = mixed[pl.ds(start, rows), q * z.elements : (q + 1) * z.elements]
            for p in range(z.quantities):
                term = value * jacobians[q, p, d : d + 1, :]
                totals[p] = term if totals[p] is None else totals[p] + term
    return totals


def full_rows(value, rows):
    short = rows - value.shape[0]
    if short == 0:
        return value
    return jnp.concatenate([value, jnp.zeros((short, value.shape[1]), value.dtype)], axis=0)


def predict(z, substep, cluster, state, jacobians, stiff, project, send_hot, outgoing, table, faces, moments, rhs, mixed, total, weights):
    e = z.elements
    for power, row in enumerate(weights_of(cluster[...], substep)):
        weights[power] = jnp.broadcast_to(row, (8, e))
    for q in range(z.quantities):
        for first, rows in z.groups():
            value = state(q, first, rows)
            total[q, first : first + rows, :] = value * weights[0, 0:1, :]
            put_halves(rhs, z.padded, first, q * e, full_rows(value, 16))

    def derivative(power, carry):
        mixed[...] = product(stiff[...], rhs[...])
        weight = weights[power]

        def group(first, rows):
            sums = contract(z, mixed, jacobians, first, rows)
            for p in range(z.quantities):
                total[p, pl.ds(first, rows), :] += sums[p] * weight[0:1, :]
                put_halves(rhs, z.padded, first, p * e, full_rows(sums[p], 16))

        by_groups(z, group)
        return carry

    lax.fori_loop(1, DERIVATIVES, derivative, 0)
    for q in range(z.quantities):
        for first, rows in z.groups():
            put_halves(moments, z.padded, first, q * e, full_rows(total[q, first : first + rows, :], 16))
    projected = product(project[...], moments[...])
    faces[...] = projected
    r = z.face_rows
    for j in range(z.faces):
        pieces = [projected[j * r : (j + 1) * r, q * e : (q + 1) * e] for q in range(z.quantities)]
        high, low = halves(full_rows(jnp.concatenate(pieces, axis=0), z.block_padded))
        table[: z.block_padded, j * e : (j + 1) * e] = high
        table[z.block_padded :, j * e : (j + 1) * e] = low
    picked = product(table[...], send_hot[...])
    for t, target in enumerate(outgoing):
        columns = slice(t * z.slots, (t + 1) * z.slots)
        target[...] = picked[: z.block, columns] + picked[z.block_padded : z.block_padded + z.block, columns]


def first_kernel(z, *refs):
    count = len(z.plan)
    outgoing = refs[8 : 8 + count]
    table, faces, moments, stiff, project, send_hot, cluster, turns = refs[8 + count : 16 + count]
    rhs, mixed, total, weights, wide_stiff, wide_project = refs[16 + count : 22 + count]
    *held, arrived = refs[22 + count :]
    held = [*held[:4], cluster, *held[4:], turns]
    copies = [pltpu.make_async_copy(refs[n], held[n], arrived.at[n]) for n in range(8)]
    for n in (5, 6, 2, 3, 4, 0, 1, 7):
        copies[n].start()
    solution, jacobians, stiffness, projection, _, send_faces, counts, _ = held
    b = z.basis
    for n in (5, 6):
        copies[n].wait()
    slot = lax.broadcasted_iota(jnp.int32, (1, z.slots), 1)
    for t, entry in enumerate(z.plan):
        chosen = lists_of(entry)[0]
        wanted = jnp.where(slot < counts[0, chosen], send_faces[pl.ds(chosen, 1), :], -1)
        send_hot[:, t * z.slots : (t + 1) * z.slots] = one_hot((z.face_total, z.slots), wanted, 0)
    for n in (2, 3, 4):
        copies[n].wait()
    stiff[...] = left_parts(wide_stiff, [(d * b, 0, -stiffness[d]) for d in range(3)], z.padded)
    project[...] = left_parts(
        wide_project, [(j * z.face_rows, 0, projection[:, j, :]) for j in range(z.faces)], z.padded
    )
    for n in (0, 1, 7):
        copies[n].wait()
    predict(
        z, 0, cluster, lambda q, k, n: solution[q, k : k + n, :], jacobians, stiff, project, send_hot,
        outgoing, table, faces, moments, rhs, mixed, total, weights,
    )


def tables_kernel(z, *refs):
    volume, lift, rotation, neighbours, orient = refs[:5]
    volume_left, lift_left, turned_left, picks, own_hot, far_hot, last_hot = refs[5:12]
    wide_volume, wide_lift, wide_turned = refs[12:]
    e, r, f = z.elements, z.face_rows, z.face_basis
    volume_left[...] = left_parts(wide_volume, [(d * z.basis, 0, volume[d]) for d in range(3)], z.padded)
    plain, turned = [], []
    for i in range(z.faces):
        face = jnp.transpose(lift[:, i, :], (1, 0))
        plain.append((0, i * r, face))
        for o in range(z.rotations):
            value = jnp.dot(face, rotation[o], precision=lax.Precision.HIGHEST, preferred_element_type=F32)
            turned.append((0, o * z.lifted + i * r, value))
    lift_left[...] = left_parts(wide_lift, plain, z.lifted)
    wide_turned[...] = jnp.zeros_like(wide_turned)
    for row, column, value in turned:
        high = value.astype(BF16).astype(F32)
        columns = slice(column, column + value.shape[1])
        wide_turned[: z.basis, columns] = high
        wide_turned[z.basis :, columns] = value - high
    turned_left[...] = wide_turned[...].astype(BF16)
    for o in range(z.rotations):
        rows = [
            jnp.broadcast_to(jnp.where(orient[i : i + 1, :] == o, 1.0, 0.0), (r, e)) for i in range(z.faces)
        ]
        picks[o] = jnp.concatenate(rows, axis=0).astype(BF16)
    for i in range(z.faces):
        wanted = neighbours[i : i + 1, :]
        own_hot[:, i * e : (i + 1) * e] = one_hot((z.face_total, e), wanted, 0)
        for t, entry in enumerate(z.plan):
            _, direction, exists = lists_of(entry)
            offset = jnp.where(exists, z.face_total + direction * z.slots, -z.slots)
            hot = one_hot((z.slots, e), wanted, offset)
            if t == len(z.plan) - 1:
                last_hot[:, i * e : (i + 1) * e] = hot
            else:
                far_hot[t * z.slots : (t + 1) * z.slots, i * e : (i + 1) * e] = hot


def solve(z, block, solver, store):
    chunk = 3 if z.quantities % 3 == 0 else 1
    together = 2 if z.faces % 2 == 0 else 1

    def some(index, carry):
        for i in range(0, z.faces, together):
            sums = [[None] * together for _ in range(chunk)]
            for q in range(z.quantities):
                for j in range(together):
                    value = block(q, i + j)
                    for c in range(chunk):
                        term = value * solver[q, index * chunk + c, i + j : i + j + 1, :]
                        sums[c][j] = term if sums[c][j] is None else sums[c][j] + term
            for c in range(chunk):
                column = pl.multiple_of((index * chunk + c) * z.elements, z.elements)
                store(i, together, column, sums[c])
        return carry

    lax.fori_loop(0, z.quantities // chunk, some, 0)


def inner_kernel(z, running, table, faces, moments, jacobians, local_solver, volume_left, lift_left, own_hot, gathered, partial, mixed, rhs):
    e, r = z.elements, z.face_rows
    picked = product(table[...], own_hot[...])
    gathered[...] = picked[: z.block, :] + picked[z.block_padded : z.block_padded + z.block, :]
    def store(i, j, p, values):
        put_halves(rhs, z.lifted, i * r, p, jnp.concatenate(values, axis=0))

    solve(z, lambda q, i: faces[i * r : (i + 1) * r, q * e : (q + 1) * e], local_solver, store)
    lifted = product(lift_left[...], rhs[...])
    for q in range(z.quantities):
        partial[q] = running[q] - lifted[:, q * e : (q + 1) * e]
    mixed[...] = product(volume_left[...], moments[...])

    def group(first, rows):
        sums = contract(z, mixed, jacobians, first, rows)
        for p in range(z.quantities):
            partial[p, pl.ds(first, rows), :] += sums[p]

    by_groups(z, group)


def received_blocks(z, incoming, gathered, far_hot, received):
    b, half = z.block, z.block_padded
    for t, source in enumerate(incoming):
        high, low = halves(full_rows(source[...], half))
        received[:half, t * z.slots : (t + 1) * z.slots] = high
        received[half:, t * z.slots : (t + 1) * z.slots] = low
    picked = product(received[...], far_hot[...])
    return gathered[...] + picked[:b, :] + picked[half : half + b, :]


def early_kernel(z, *refs):
    *incoming, gathered, far_hot, blocks, received = refs
    blocks[...] = received_blocks(z, incoming, gathered, far_hot, received)


def neighbour_flux(z, incoming, gathered, neighbour_solver, picks, far_hot, turned_left, received, blocks, turned):
    e, r = z.elements, z.face_rows
    blocks[...] = received_blocks(z, [incoming], gathered, far_hot, received)
    width = z.rotations * z.lifted

    def store(i, together, column, values):
        high, low = halves(jnp.concatenate(values, axis=0))
        rows = together * r
        for o in range(z.rotations):
            pick = picks[o, i * r : i * r + rows, :]
            row = o * z.lifted + i * r
            turned[row : row + rows, pl.ds(column, e)] = high * pick
            turned[width + row : width + row + rows, pl.ds(column, e)] = low * pick

    solve(z, lambda q, i: blocks[q * r : (q + 1) * r, i * e : (i + 1) * e], neighbour_solver, store)
    both = product(turned_left[...], turned[:width, :])
    return both[: z.basis, :] + both[z.basis :, :] + product(turned_left[: z.basis, :], turned[width:, :])


def outer_kernel(z, substep, *refs):
    count = len(z.plan)
    incoming = refs[0]
    (gathered, partial, solution, neighbour_solver, picks, far_hot, turned_left, jacobians, stiff, project, send_hot, cluster) = refs[
        1:13
    ]
    outgoing = refs[13 : 13 + count]
    table, faces, moments, updated, running = refs[13 + count : 18 + count]
    rhs, mixed, total, weights, received, blocks, turned = refs[18 + count :]
    e = z.elements
    flux = neighbour_flux(
        z, incoming, gathered, neighbour_solver, picks, far_hot, turned_left, received, blocks, turned
    )
    ending = ((substep + 1) & (period_of(cluster[...]) - 1)) == 0
    for q in range(z.quantities):
        value = partial[q] - flux[:, q * e : (q + 1) * e]
        running[q] = value
        updated[q] = jnp.where(ending, value, solution[q])
    predict(
        z, substep + 1, cluster, lambda q, k, n: updated[q, k : k + n, :], jacobians, stiff, project, send_hot,
        outgoing, table, faces, moments, rhs, mixed, total, weights,
    )


def last_kernel(z, *refs):
    incoming, gathered, partial, neighbour_solver, picks, far_hot, turned_left, advanced, received, blocks, turned = refs
    e = z.elements
    flux = neighbour_flux(
        z, incoming, gathered, neighbour_solver, picks, far_hot, turned_left, received, blocks, turned
    )
    for q in range(z.quantities):
        advanced[q] = partial[q] - flux[:, q * e : (q + 1) * e]


def call(body, outs, scratch, cost, arguments, space=pltpu.VMEM, more=()):
    in_specs = [pl.BlockSpec(memory_space=space)] * len(arguments)
    return pl.pallas_call(
        body,
        out_shape=[jax.ShapeDtypeStruct(shape, kind) for shape, kind in outs],
        in_specs=in_specs,
        out_specs=[pl.BlockSpec(memory_space=pltpu.VMEM)] * len(outs),
        scratch_shapes=[*(pltpu.VMEM(shape, kind) for shape, kind in scratch), *more],
        cost_estimate=pl.CostEstimate(flops=cost, bytes_accessed=1 << 20, transcendentals=0),
        compiler_params=pltpu.CompilerParams(vmem_limit_bytes=24 << 20),
    )(*arguments)


def local(
    plan,
    solution,
    jacobians,
    derivative_stiffness,
    volume_stiffness,
    face_project,
    face_lift,
    face_rotation,
    local_solver,
    neighbour_solver,
    cluster,
    neighbours,
    orient,
    send_faces,
    counts,
):
    z = Sizes(solution, face_project, send_faces, plan)
    count = len(plan)
    sizes = [lax.axis_size(axis) for axis in AXES]
    state = solution.transpose(1, 0, 2)
    jacobians = jacobians.transpose(1, 2, 0, 3)
    local_solver = local_solver.transpose(1, 2, 0, 3)
    neighbour_solver = neighbour_solver.transpose(1, 2, 0, 3)
    projection = face_project.transpose(1, 0, 2)
    lift = face_lift.transpose(2, 0, 1)
    cluster = cluster.reshape(1, -1)
    counts = counts.reshape(1, -1)

    block = ((z.block, z.slots), F32)
    table = ((2 * z.block_padded, z.face_total), BF16)
    faces = ((z.lifted, z.columns), F32)
    moments = ((3 * z.padded, z.columns), BF16)
    stiff = ((3 * z.basis, 3 * z.padded), BF16)
    project = ((z.lifted, 3 * z.padded), BF16)
    field = ((z.quantities, z.basis, z.elements), F32)
    gathered = ((z.block, z.face_total), F32)
    send_hot = ((z.face_total, count * z.slots), BF16)
    far_hot = (((count - 1) * z.slots, z.face_total), BF16)
    last_hot = ((z.slots, z.face_total), BF16)
    own_hot = ((z.face_total, z.face_total), BF16)
    lift_left = ((z.basis, 3 * z.lifted), BF16)
    turned_left = ((2 * z.basis, z.rotations * z.lifted), BF16)
    picks = ((z.rotations, z.lifted, z.elements), BF16)
    mixed = ((3 * z.basis, z.columns), F32)
    weights = ((DERIVATIVES, 8, z.elements), F32)
    received = ((2 * z.block_padded, (count - 1) * z.slots), BF16)
    last_received = ((2 * z.block_padded, z.slots), BF16)
    turned = ((2 * z.rotations * z.lifted, z.columns), BF16)

    def wide(entry):
        return (entry[0], F32)

    def trade(outgoing):
        return [
            lax.ppermute(value, AXES, partners(sizes, entry)) for value, entry in zip(outgoing, plan)
        ]

    first_arguments = tuple(
        pltpu.with_memory_space_constraint(value, pltpu.HBM)
        for value in (
            state, jacobians, derivative_stiffness, projection, cluster, send_faces, counts, face_rotation,
        )
    )
    results = call(
        functools.partial(first_kernel, z),
        [block] * count
        + [table, faces, moments, stiff, project, send_hot]
        + [(value.shape, value.dtype) for value in (cluster, face_rotation)],
        [moments, mixed, field, weights, wide(stiff), wide(project)],
        10_000_000,
        first_arguments,
        space=pltpu.HBM,
        more=[
            *(pltpu.VMEM(value.shape, value.dtype) for value in (*first_arguments[:4], send_faces)),
            pltpu.SMEM(counts.shape, counts.dtype),
            pltpu.SemaphoreType.DMA((len(first_arguments),)),
        ],
    )
    outgoing = results[:count]
    table_now, faces_now, moments_now, stiff_left, project_left, send_matrix, cluster, turns = results[count:]
    running = state
    for substep in range(SUBSTEPS):
        incoming = trade(outgoing)
        if substep == 0:
            volume_left, lift_plain, lift_turned, orient_picks, own_matrix, far_matrix, last_matrix = call(
                functools.partial(tables_kernel, z),
                [stiff, lift_left, turned_left, picks, own_hot, far_hot, last_hot],
                [wide(stiff), wide(lift_left), wide(turned_left)],
                1_000_000,
                (volume_stiffness, lift, turns, neighbours, orient),
            )
        gathered_now, partial = call(
            functools.partial(inner_kernel, z),
            [gathered, field],
            [mixed, ((3 * z.lifted, z.columns), BF16)],
            10_000_000,
            (running, table_now, faces_now, moments_now, jacobians, local_solver, volume_left, lift_plain, own_matrix),
        )
        (gathered_now,) = call(
            functools.partial(early_kernel, z),
            [gathered],
            [received],
            5_000_000,
            (*incoming[:-1], gathered_now, far_matrix),
        )
        if substep == SUBSTEPS - 1:
            (advanced,) = call(
                functools.partial(last_kernel, z),
                [field],
                [last_received, gathered, turned],
                10_000_000,
                (incoming[-1], gathered_now, partial, neighbour_solver, orient_picks, last_matrix, lift_turned),
            )
            return advanced.transpose(1, 0, 2)
        results = call(
            functools.partial(outer_kernel, z, substep),
            [block] * count + [table, faces, moments, field, field],
            [moments, mixed, field, weights, last_received, gathered, turned],
            10_000_000,
            (
                incoming[-1], gathered_now, partial, state, neighbour_solver, orient_picks, last_matrix, lift_turned,
                jacobians, stiff_left, project_left, send_matrix, cluster,
            ),
        )
        outgoing = results[:count]
        table_now, faces_now, moments_now, state, running = results[count:]


def solution(mesh):
    spread = ("gx", "gy", "gz")
    return jax.shard_map(
        functools.partial(local, exchange_plan(mesh)),
        mesh=mesh,
        in_specs=(
            P(None, None, spread),
            P(None, None, None, spread),
            P(),
            P(),
            P(),
            P(),
            P(),
            P(None, None, None, spread),
            P(None, None, None, spread),
            P(spread),
            P(None, spread),
            P(None, spread),
            P(None, spread),
            P(None, spread),
        ),
        out_specs=P(None, None, spread),
        check_vma=False,
    )
```

```python
import functools
import math

import jax
import jax.numpy as jnp
from jax import lax
from jax.experimental import pallas as pl
from jax.experimental.pallas import tpu as pltpu
from jax.sharding import PartitionSpec as P

DERIVATIVES = 6
SUBSTEPS = 4
SPAN = 1.0
F32 = jnp.float32
BF16 = jnp.bfloat16
AXES = ("gx", "gy", "gz")


def rounded(size, unit):
    return -(-size // unit) * unit


def halves(value):
    high = value.astype(BF16)
    return high, (value - high.astype(F32)).astype(BF16)


def product(left, right):
    return jnp.dot(left, right, preferred_element_type=F32)


def exchange_plan(mesh):
    plan = []
    for number, axis in enumerate(AXES):
        size = mesh.shape[axis]
        if size == 1:
            continue
        if size == 2:
            plan.append((number, size, "pair0"))
        elif size % 2 == 0:
            plan.append((number, size, "pair0"))
            plan.append((number, size, "pair1"))
        else:
            plan.append((number, size, "up"))
            plan.append((number, size, "down"))
    return tuple(plan)


def partners(sizes, entry):
    number, size, kind = entry
    spare = [other for other in (2, 0, 1) if other != number and sizes[other] % 2 == 0]
    pairs = []
    for flat in range(math.prod(sizes)):
        place = [flat // (sizes[1] * sizes[2]), flat // sizes[2] % sizes[1], flat % sizes[2]]
        source = flat
        here = place[number]
        if kind in ("up", "down"):
            place[number] = (here + (1 if kind == "up" else -1)) % size
        elif kind == "pair0":
            place[number] = here ^ 1
        elif 0 < here < size - 1:
            place[number] = ((here + 1) ^ 1) - 1
        elif spare:
            place[spare[0]] ^= 1
        else:
            place[number] = size - 1 - here
        pairs.append((source, (place[0] * sizes[1] + place[1]) * sizes[2] + place[2]))
    return pairs


def lists_of(entry):
    number, size, kind = entry
    place = lax.axis_index(AXES[number])
    if kind == "up":
        return 2 * number, 2 * number, place > 0
    if kind == "down":
        return 2 * number + 1, 2 * number + 1, place < size - 1
    parity = lax.rem(place, 2)
    upper = parity if kind == "pair0" else 1 - parity
    exists = jnp.where(upper == 1, place > 0, place < size - 1)
    return 2 * number + upper, 2 * number + 1 - upper, exists


class Sizes:
    def __init__(self, solution, face_project, send_faces, plan):
        self.basis, self.quantities, self.elements = solution.shape
        self.faces, self.face_basis, _ = face_project.shape
        self.slots = send_faces.shape[1]
        self.plan = plan
        self.padded = rounded(self.basis, 16)
        self.face_rows = rounded(self.face_basis, 8)
        self.block = self.quantities * self.face_rows
        self.block_padded = rounded(self.block, 16)
        self.columns = self.quantities * self.elements
        self.face_total = self.faces * self.elements
        self.lifted = self.faces * self.face_rows
        self.rotations = 3
        count = len(plan)
        self.by_product = count - 1 if count % 2 and count > 1 and self.elements == 128 else count
        self.chunk = 3 if self.quantities % 3 == 0 else 1

    def groups(self):
        return [(k, min(16, self.basis - k)) for k in range(0, self.basis, 16)]


def left_parts(scratch, pieces, width):
    scratch[...] = jnp.zeros_like(scratch)
    for row, column, value in pieces:
        high = value.astype(BF16).astype(F32)
        rows, columns = value.shape
        scratch[row : row + rows, column : column + columns] = high
        scratch[row : row + rows, width + column : width + column + columns] = high
        scratch[row : row + rows, 2 * width + column : 2 * width + column + columns] = value - high
    return scratch[...].astype(BF16)


def one_hot(shape, targets, offset):
    rows = lax.broadcasted_iota(jnp.int32, shape, 0)
    return jnp.where(rows == targets - offset, 1.0, 0.0).astype(BF16)


def period_of(cluster):
    return jnp.left_shift(jnp.ones_like(cluster), cluster)


def weights_of(cluster, substep):
    offset = (substep & (period_of(cluster) - 1)).astype(F32)
    step = SPAN / SUBSTEPS
    upper, lower = (offset + 1.0) * step, offset * step
    rows, high, low = [], upper, lower
    for power in range(DERIVATIVES):
        rows.append((high - low) * (1.0 / math.factorial(power + 1)))
        high, low = high * upper, low * lower
    return rows


def put_halves(target, width, row, column, value):
    high, low = halves(value)
    rows, columns = value.shape
    for part, piece in enumerate((high, low, high)):
        start = part * width + row
        if not isinstance(row, int):
            start = pl.multiple_of(start, 16)
        target[pl.ds(start, rows), pl.ds(column, columns)] = piece


def by_groups(z, group):
    whole = z.basis // 16
    group(0, 16)

    def later(index, carry):
        group(pl.multiple_of(index * 16, 16), 16)
        return carry

    lax.fori_loop(1, whole, later, 0)
    if z.basis % 16:
        group(whole * 16, z.basis % 16)


def contract(z, mixed, jacobians, first, rows):
    totals = [None] * z.quantities
    for q in range(z.quantities):
        for d in range(3):
            start = d * z.basis + first
            value = mixed[pl.ds(start, rows), q * z.elements : (q + 1) * z.elements]
            for p in range(z.quantities):
                term = value * jacobians[q, p, d : d + 1, :]
                totals[p] = term if totals[p] is None else totals[p] + term
    return totals


def full_rows(value, rows):
    short = rows - value.shape[0]
    if short == 0:
        return value
    return jnp.concatenate([value, jnp.zeros((short, value.shape[1]), value.dtype)], axis=0)


def weight_rows(z, substep, cluster, weights):
    for power, row in enumerate(weights_of(cluster[...], substep)):
        weights[power] = jnp.broadcast_to(row, (8, z.elements))


def predictor_kernel(z, state, jacobians, stiff, weights, moments, rhs, mixed, total):
    e = z.elements
    for q in range(z.quantities):
        for first, rows in z.groups():
            value = state[q, first : first + rows, :]
            total[q, first : first + rows, :] = value * weights[0, 0:1, :]
            put_halves(rhs, z.padded, first, q * e, full_rows(value, 16))

    def derivative(power, carry):
        mixed[...] = product(stiff[...], rhs[...])
        weight = weights[power]

        def group(first, rows):
            sums = contract(z, mixed, jacobians, first, rows)
            for p in range(z.quantities):
                total[p, pl.ds(first, rows), :] += sums[p] * weight[0:1, :]
                put_halves(rhs, z.padded, first, p * e, full_rows(sums[p], 16))

        by_groups(z, group)
        return carry

    lax.fori_loop(1, DERIVATIVES, derivative, 0)
    for q in range(z.quantities):
        for first, rows in z.groups():
            put_halves(moments, z.padded, first, q * e, full_rows(total[q, first : first + rows, :], 16))


def along_lanes(blocks, wanted, elements):
    face, lane = wanted >> (elements.bit_length() - 1), wanted & (elements - 1)
    result = []
    for rows in zip(*blocks):
        picked = jnp.zeros_like(rows[0])
        for j, row in enumerate(rows):
            shape = row.shape
            taken = jnp.take_along_axis(row, jnp.broadcast_to(lane, shape), axis=1, mode="promise_in_bounds")
            picked = jnp.where(jnp.broadcast_to(face == j, shape), taken, picked)
        result.append(picked)
    return result


def dense_rows(z, target, value):
    for q in range(z.quantities):
        target[q * z.face_basis : q * z.face_basis + z.face_rows, :] = value[q * z.face_rows : (q + 1) * z.face_rows]


def send_kernel(z, moments, project, send_hot, send_last, *refs):
    count = len(z.plan)
    outgoing = refs[:count]
    table, faces = refs[count:]
    e, r, half = z.elements, z.face_rows, z.block_padded
    projected = product(project[...], moments[...])
    faces[...] = projected
    blocks = []
    for j in range(z.faces):
        pieces = [projected[j * r : (j + 1) * r, q * e : (q + 1) * e] for q in range(z.quantities)]
        blocks.append([piece[k : k + 8] for piece in pieces for k in range(0, r, 8)])
        high, low = halves(full_rows(jnp.concatenate(pieces, axis=0), half))
        table[:half, j * e : (j + 1) * e] = high
        table[half:, j * e : (j + 1) * e] = low
    by_product = z.by_product
    if by_product:
        picked = product(table[...], send_hot[...])
        for t in range(by_product):
            columns = slice(t * z.slots, (t + 1) * z.slots)
            dense_rows(z, outgoing[t], picked[: z.block, columns] + picked[half : half + z.block, columns])
    for t in range(by_product, count):
        rows = along_lanes(blocks, send_last[t - by_product : t - by_product + 1, :], e)
        dense_rows(z, outgoing[t], jnp.concatenate(rows, axis=0))


def first_kernel(z, *refs):
    given = refs[:8]
    state, jacobians, cluster, turns, stiff, project, send_hot, send_last, weights = refs[8:17]
    wide_stiff, wide_project, stiffness, projection, lists, sizes, arrived = refs[17:]
    targets = [state, jacobians, stiffness, projection, cluster, turns, lists, sizes]
    copies = [pltpu.make_async_copy(given[n], targets[n], arrived.at[n]) for n in range(8)]
    for n in (6, 7, 2, 3, 4, 5, 0, 1):
        copies[n].start()
    b = z.basis
    for n in (6, 7):
        copies[n].wait()
    slot = lax.broadcasted_iota(jnp.int32, (1, z.slots), 1)
    for t, entry in enumerate(z.plan):
        chosen = lists_of(entry)[0]
        wanted = jnp.where(slot < sizes[0, chosen], lists[pl.ds(chosen, 1), :], -1)
        if t < z.by_product:
            send_hot[:, t * z.slots : (t + 1) * z.slots] = one_hot((z.face_total, z.slots), wanted, 0)
        else:
            send_last[t - z.by_product : t - z.by_product + 1, :] = wanted
    for n in (2, 3, 4):
        copies[n].wait()
    weight_rows(z, 0, cluster, weights)
    stiff[...] = left_parts(wide_stiff, [(d * b, 0, -stiffness[d]) for d in range(3)], z.padded)
    project[...] = left_parts(
        wide_project, [(j * z.face_rows, 0, projection[:, j, :]) for j in range(z.faces)], z.padded
    )
    for n in (5, 0, 1):
        copies[n].wait()


def tables_kernel(z, *refs):
    volume, lift, rotation, neighbours, orient = refs[:5]
    volume_left, lift_left, turned_left, picks, own_hot, far_hot, last_hot = refs[5:12]
    wide_volume, wide_lift, wide_turned = refs[12:]
    e, r, f = z.elements, z.face_rows, z.face_basis
    volume_left[...] = left_parts(wide_volume, [(d * z.basis, 0, volume[d]) for d in range(3)], z.padded)
    plain, turned = [], []
    for i in range(z.faces):
        face = jnp.transpose(lift[:, i, :], (1, 0))
        plain.append((0, i * r, face))
        for o in range(z.rotations):
            value = jnp.dot(face, rotation[o], precision=lax.Precision.HIGHEST, preferred_element_type=F32)
            turned.append((0, o * z.lifted + i * r, value))
    lift_left[...] = left_parts(wide_lift, plain, z.lifted)
    wide_turned[...] = jnp.zeros_like(wide_turned)
    for row, column, value in turned:
        high = value.astype(BF16).astype(F32)
        columns = slice(column, column + value.shape[1])
        wide_turned[: z.basis, columns] = high
        wide_turned[z.basis :, columns] = value - high
    turned_left[...] = wide_turned[...].astype(BF16)
    for o in range(z.rotations):
        rows = [
            jnp.broadcast_to(jnp.where(orient[i : i + 1, :] == o, 1.0, 0.0), (r, e)) for i in range(z.faces)
        ]
        picks[o] = jnp.concatenate(rows, axis=0).astype(BF16)
    for i in range(z.faces):
        wanted = neighbours[i : i + 1, :]
        own_hot[:, i * e : (i + 1) * e] = one_hot((z.face_total, e), wanted, 0)
        for t, entry in enumerate(z.plan):
            _, direction, exists = lists_of(entry)
            offset = jnp.where(exists, z.face_total + direction * z.slots, -z.slots)
            hot = one_hot((z.slots, e), wanted, offset)
            if t == len(z.plan) - 1:
                last_hot[:, i * e : (i + 1) * e] = hot
            else:
                far_hot[t * z.slots : (t + 1) * z.slots, i * e : (i + 1) * e] = hot


def solve(z, index, block, solver, store):
    together = 2 if z.faces % 2 == 0 else 1
    for i in range(0, z.faces, together):
        sums = [[None] * together for _ in range(z.chunk)]
        for q in range(z.quantities):
            for j in range(together):
                value = block(q, i + j)
                for c in range(z.chunk):
                    term = value * solver[q, index * z.chunk + c, i + j : i + j + 1, :]
                    sums[c][j] = term if sums[c][j] is None else sums[c][j] + term
        for c in range(z.chunk):
            column = (index * z.chunk + c) * z.elements
            if not isinstance(column, int):
                column = pl.multiple_of(column, z.elements)
            store(i, together, column, sums[c])


def inner_kernel(z, running, table, faces, moments, jacobians, local_solver, volume_left, lift_left, own_hot, gathered, partial, mixed, rhs):
    e, r = z.elements, z.face_rows
    picked = product(table[...], own_hot[...])
    gathered[...] = picked[: z.block, :] + picked[z.block_padded : z.block_padded + z.block, :]
    def store(i, j, p, values):
        put_halves(rhs, z.lifted, i * r, p, jnp.concatenate(values, axis=0))

    def some(index, carry):
        solve(z, index, lambda q, i: faces[i * r : (i + 1) * r, q * e : (q + 1) * e], local_solver, store)
        return carry

    lax.fori_loop(0, z.quantities // z.chunk, some, 0)
    lifted = product(lift_left[...], rhs[...])
    for q in range(z.quantities):
        partial[q] = running[q] - lifted[:, q * e : (q + 1) * e]
    mixed[...] = product(volume_left[...], moments[...])

    def group(first, rows):
        sums = contract(z, mixed, jacobians, first, rows)
        for p in range(z.quantities):
            partial[p, pl.ds(first, rows), :] += sums[p]

    by_groups(z, group)


def received_blocks(z, incoming, gathered, far_hot, received):
    b, half = z.block, z.block_padded
    for t, source in enumerate(incoming):
        pieces = [source[q * z.face_basis : q * z.face_basis + z.face_rows, :] for q in range(z.quantities)]
        high, low = halves(full_rows(jnp.concatenate(pieces, axis=0), half))
        received[:half, t * z.slots : (t + 1) * z.slots] = high
        received[half:, t * z.slots : (t + 1) * z.slots] = low
    picked = product(received[...], far_hot[...])
    return gathered[...] + picked[:b, :] + picked[half : half + b, :]


def early_kernel(z, *refs):
    *incoming, gathered, far_hot, blocks, received = refs
    blocks[...] = received_blocks(z, incoming, gathered, far_hot, received)


def neighbour_flux(z, incoming, gathered, neighbour_solver, picks, far_hot, turned_left, received, blocks, turned, take):
    e, r, b = z.elements, z.face_rows, z.basis
    blocks[...] = received_blocks(z, [incoming], gathered, far_hot, received)
    width = z.rotations * z.lifted

    def store(i, together, column, values):
        high, low = halves(jnp.concatenate(values, axis=0))
        rows = together * r
        for o in range(z.rotations):
            pick = picks[o, i * r : i * r + rows, :]
            row = o * z.lifted + i * r
            turned[row : row + rows, pl.ds(column, e)] = high * pick
            turned[width + row : width + row + rows, pl.ds(column, e)] = low * pick

    def some(index, carry):
        solve(z, index, lambda q, i: blocks[q * r : (q + 1) * r, i * e : (i + 1) * e], neighbour_solver, store)
        return carry

    lax.fori_loop(0, z.quantities // z.chunk, some, 0)
    both = product(turned_left[...], turned[:width, :])
    flux = both[:b, :] + both[b:, :] + product(turned_left[:b, :], turned[width:, :])
    for q in range(z.quantities):
        take(q, flux[:, q * e : (q + 1) * e])


def flux_kernel(z, substep, *refs):
    (incoming, gathered, partial, solution, neighbour_solver, picks, far_hot, turned_left, cluster) = refs[:9]
    updated, running, weights, received, blocks, turned = refs[9:]
    weight_rows(z, substep + 1, cluster, weights)
    ending = ((substep + 1) & (period_of(cluster[...]) - 1)) == 0

    def take(q, flux):
        value = partial[q] - flux
        running[q] = value
        updated[q] = jnp.where(ending, value, solution[q])

    neighbour_flux(
        z, incoming, gathered, neighbour_solver, picks, far_hot, turned_left, received, blocks, turned, take
    )


def last_kernel(z, *refs):
    (incoming, gathered, partial, neighbour_solver, picks, far_hot, turned_left) = refs[:7]
    advanced, received, blocks, turned, done, sent = refs[7:]
    groups = z.quantities // z.chunk

    def copy(index):
        part = pl.ds(index * z.chunk, z.chunk)
        return pltpu.make_async_copy(done.at[part], advanced.at[part], sent.at[index])

    def take(q, flux):
        done[q] = partial[q] - flux

    neighbour_flux(
        z, incoming, gathered, neighbour_solver, picks, far_hot, turned_left, received, blocks, turned, take
    )
    for index in range(groups):
        copy(index).start()
    for index in range(groups):
        copy(index).wait()


def call(body, outs, scratch, cost, arguments, space=pltpu.VMEM, out_space=pltpu.VMEM, more=(), flags=None):
    in_specs = [pl.BlockSpec(memory_space=space)] * len(arguments)
    return pl.pallas_call(
        body,
        out_shape=[jax.ShapeDtypeStruct(shape, kind) for shape, kind in outs],
        in_specs=in_specs,
        out_specs=[pl.BlockSpec(memory_space=out_space)] * len(outs),
        scratch_shapes=[*(pltpu.VMEM(shape, kind) for shape, kind in scratch), *more],
        cost_estimate=pl.CostEstimate(flops=cost, bytes_accessed=1 << 20, transcendentals=0),
        compiler_params=pltpu.CompilerParams(vmem_limit_bytes=24 << 20, flags=flags or {}),
    )(*arguments)


def local(
    plan,
    solution,
    jacobians,
    derivative_stiffness,
    volume_stiffness,
    face_project,
    face_lift,
    face_rotation,
    local_solver,
    neighbour_solver,
    cluster,
    neighbours,
    orient,
    send_faces,
    counts,
):
    z = Sizes(solution, face_project, send_faces, plan)
    count = len(plan)
    sizes = [lax.axis_size(axis) for axis in AXES]
    state = solution.transpose(1, 0, 2)
    jacobians = jacobians.transpose(1, 2, 0, 3)
    local_solver = local_solver.transpose(1, 2, 0, 3)
    neighbour_solver = neighbour_solver.transpose(1, 2, 0, 3)
    projection = face_project.transpose(1, 0, 2)
    lift = face_lift.transpose(2, 0, 1)
    cluster = cluster.reshape(1, -1)
    counts = counts.reshape(1, -1)

    block = (((z.quantities - 1) * z.face_basis + z.face_rows, z.slots), F32)
    table = ((2 * z.block_padded, z.face_total), BF16)
    faces = ((z.lifted, z.columns), F32)
    moments = ((3 * z.padded, z.columns), BF16)
    stiff = ((3 * z.basis, 3 * z.padded), BF16)
    project = ((z.lifted, 3 * z.padded), BF16)
    field = ((z.quantities, z.basis, z.elements), F32)
    gathered = ((z.block, z.face_total), F32)
    send_hot = ((z.face_total, max(1, z.by_product) * z.slots), BF16)
    send_last = ((max(1, count - z.by_product), z.slots), jnp.int32)
    far_hot = (((count - 1) * z.slots, z.face_total), BF16)
    last_hot = ((z.slots, z.face_total), BF16)
    own_hot = ((z.face_total, z.face_total), BF16)
    lift_left = ((z.basis, 3 * z.lifted), BF16)
    turned_left = ((2 * z.basis, z.rotations * z.lifted), BF16)
    picks = ((z.rotations, z.lifted, z.elements), BF16)
    mixed = ((3 * z.basis, z.columns), F32)
    weights = ((DERIVATIVES, 8, z.elements), F32)
    received = ((2 * z.block_padded, (count - 1) * z.slots), BF16)
    last_received = ((2 * z.block_padded, z.slots), BF16)
    turned = ((2 * z.rotations * z.lifted, z.columns), BF16)

    def wide(entry):
        return (entry[0], F32)

    given = (
        state, jacobians, derivative_stiffness, projection, cluster, face_rotation, send_faces, counts,
    )
    results = call(
        functools.partial(first_kernel, z),
        [(given[n].shape, given[n].dtype) for n in (0, 1, 4, 5)] + [stiff, project, send_hot, send_last, weights],
        [wide(stiff), wide(project)],
        1_000_000,
        tuple(pltpu.with_memory_space_constraint(value, pltpu.HBM) for value in given),
        space=pltpu.HBM,
        more=[
            *(pltpu.VMEM(given[n].shape, given[n].dtype) for n in (2, 3, 6)),
            pltpu.SMEM(counts.shape, counts.dtype),
            pltpu.SemaphoreType.DMA((len(given),)),
        ],
    )
    state, jacobians, cluster, turns, stiff_left, project_left, send_matrix, send_rest, weights_now = results
    running = state
    for substep in range(SUBSTEPS):
        (moments_now,) = call(
            functools.partial(predictor_kernel, z),
            [moments],
            [moments, mixed, field],
            10_000_000,
            (state, jacobians, stiff_left, weights_now),
        )
        *outgoing, table_now, faces_now = call(
            functools.partial(send_kernel, z),
            [block] * count + [table, faces],
            [],
            5_000_000,
            (moments_now, project_left, send_matrix, send_rest),
        )
        incoming = [lax.ppermute(value, AXES, partners(sizes, entry)) for value, entry in zip(outgoing, plan)]
        if substep == 0:
            volume_left, lift_plain, lift_turned, orient_picks, own_matrix, far_matrix, last_matrix = call(
                functools.partial(tables_kernel, z),
                [stiff, lift_left, turned_left, picks, own_hot, far_hot, last_hot],
                [wide(stiff), wide(lift_left), wide(turned_left)],
                1_000_000,
                (volume_stiffness, lift, turns, neighbours, orient),
            )
        gathered_now, partial = call(
            functools.partial(inner_kernel, z),
            [gathered, field],
            [mixed, ((3 * z.lifted, z.columns), BF16)],
            10_000_000,
            (running, table_now, faces_now, moments_now, jacobians, local_solver, volume_left, lift_plain, own_matrix),
        )
        (gathered_now,) = call(
            functools.partial(early_kernel, z),
            [gathered],
            [received],
            5_000_000,
            (*incoming[:-1], gathered_now, far_matrix),
        )
        if substep == SUBSTEPS - 1:
            (advanced,) = call(
                functools.partial(last_kernel, z),
                [field],
                [last_received, gathered, turned, field],
                10_000_000,
                (incoming[-1], gathered_now, partial, neighbour_solver, orient_picks, last_matrix, lift_turned),
                out_space=pltpu.HBM,
                more=[pltpu.SemaphoreType.DMA((z.quantities // z.chunk,))],
            )
            return advanced.transpose(1, 0, 2)
        state, running, weights_now = call(
            functools.partial(flux_kernel, z, substep),
            [field, field, weights],
            [last_received, gathered, turned],
            10_000_000,
            (
                incoming[-1], gathered_now, partial, state, neighbour_solver, orient_picks, last_matrix, lift_turned,
                cluster,
            ),
        )


def solution(mesh):
    spread = ("gx", "gy", "gz")
    return jax.shard_map(
        functools.partial(local, exchange_plan(mesh)),
        mesh=mesh,
        in_specs=(
            P(None, None, spread),
            P(None, None, None, spread),
            P(),
            P(),
            P(),
            P(),
            P(),
            P(None, None, None, spread),
            P(None, None, None, spread),
            P(spread),
            P(None, spread),
            P(None, spread),
            P(None, spread),
            P(None, spread),
        ),
        out_specs=P(None, None, spread),
        check_vma=False,
    )
```

```python
import functools
import math

import jax
import jax.numpy as jnp
from jax import lax
from jax.experimental import pallas as pl
from jax.experimental.pallas import tpu as pltpu
from jax.sharding import PartitionSpec as P

DERIVATIVES = 6
SUBSTEPS = 4
SPAN = 1.0
F32 = jnp.float32
BF16 = jnp.bfloat16
AXES = ("gx", "gy", "gz")


def rounded(size, unit):
    return -(-size // unit) * unit


def halves(value):
    high = value.astype(BF16)
    return high, (value - high.astype(F32)).astype(BF16)


def product(left, right):
    return jnp.dot(left, right, preferred_element_type=F32)


def exchange_plan(mesh):
    plan = []
    for number, axis in enumerate(AXES):
        size = mesh.shape[axis]
        if size == 1:
            continue
        if size == 2:
            plan.append((number, size, "pair0"))
        elif size % 2 == 0:
            plan.append((number, size, "pair0"))
            plan.append((number, size, "pair1"))
        else:
            plan.append((number, size, "up"))
            plan.append((number, size, "down"))
    near = [entry for entry in plan if entry[2] != "pair1"]
    return tuple(near + [entry for entry in plan if entry[2] == "pair1"])


def partners(sizes, entry):
    number, size, kind = entry
    spare = [other for other in (2, 0, 1) if other != number and sizes[other] % 2 == 0]
    pairs = []
    for flat in range(math.prod(sizes)):
        place = [flat // (sizes[1] * sizes[2]), flat // sizes[2] % sizes[1], flat % sizes[2]]
        source = flat
        here = place[number]
        if kind in ("up", "down"):
            place[number] = (here + (1 if kind == "up" else -1)) % size
        elif kind == "pair0":
            place[number] = here ^ 1
        elif 0 < here < size - 1:
            place[number] = ((here + 1) ^ 1) - 1
        elif spare:
            place[spare[0]] ^= 1
        else:
            place[number] = size - 1 - here
        pairs.append((source, (place[0] * sizes[1] + place[1]) * sizes[2] + place[2]))
    return pairs


def lists_of(entry):
    number, size, kind = entry
    place = lax.axis_index(AXES[number])
    if kind == "up":
        return 2 * number, 2 * number, place > 0
    if kind == "down":
        return 2 * number + 1, 2 * number + 1, place < size - 1
    parity = lax.rem(place, 2)
    upper = parity if kind == "pair0" else 1 - parity
    exists = jnp.where(upper == 1, place > 0, place < size - 1)
    return 2 * number + upper, 2 * number + 1 - upper, exists


class Sizes:
    def __init__(self, solution, face_project, send_faces, plan):
        self.basis, self.quantities, self.elements = solution.shape
        self.faces, self.face_basis, _ = face_project.shape
        self.slots = send_faces.shape[1]
        self.plan = plan
        self.padded = rounded(self.basis, 16)
        self.face_rows = rounded(self.face_basis, 8)
        self.block = self.quantities * self.face_rows
        self.block_padded = rounded(self.block, 16)
        self.columns = self.quantities * self.elements
        self.face_total = self.faces * self.elements
        self.lifted = self.faces * self.face_rows
        self.rotations = 3
        count = len(plan)
        self.by_product = count - 1 if count % 2 and count > 1 and self.elements == 128 else count
        self.late = min(2, count - 1) if count > 1 else 0
        self.early = count - self.late
        self.chunk = 3 if self.quantities % 3 == 0 else 1

    def groups(self):
        return [(k, min(16, self.basis - k)) for k in range(0, self.basis, 16)]


def left_parts(scratch, pieces, width):
    scratch[...] = jnp.zeros_like(scratch)
    for row, column, value in pieces:
        high = value.astype(BF16).astype(F32)
        rows, columns = value.shape
        scratch[row : row + rows, column : column + columns] = high
        scratch[row : row + rows, width + column : width + column + columns] = high
        scratch[row : row + rows, 2 * width + column : 2 * width + column + columns] = value - high
    return scratch[...].astype(BF16)


def stiffness_rows(z, matrices, sign):
    pieces = []
    for first, rows in z.groups():
        for d in range(3):
            pieces.append((3 * first + d * rows, 0, sign * matrices[d, first : first + rows, :]))
    return pieces


def one_hot(shape, targets, offset):
    rows = lax.broadcasted_iota(jnp.int32, shape, 0)
    return jnp.where(rows == targets - offset, 1.0, 0.0).astype(BF16)


def period_of(cluster):
    return jnp.left_shift(jnp.ones_like(cluster), cluster)


def weights_of(cluster, substep):
    offset = (substep & (period_of(cluster) - 1)).astype(F32)
    step = SPAN / SUBSTEPS
    upper, lower = (offset + 1.0) * step, offset * step
    rows, high, low = [], upper, lower
    for power in range(DERIVATIVES):
        rows.append((high - low) * (1.0 / math.factorial(power + 1)))
        high, low = high * upper, low * lower
    return rows


def put_halves(target, width, row, column, value):
    high, low = halves(value)
    rows, columns = value.shape
    for part, piece in enumerate((high, low, high)):
        start = part * width + row
        if not isinstance(row, int):
            start = pl.multiple_of(start, 16)
        target[pl.ds(start, rows), pl.ds(column, columns)] = piece


def by_groups(z, group):
    whole = z.basis // 16
    group(0, 16)

    def later(index, carry):
        group(pl.multiple_of(index * 16, 16), 16)
        return carry

    lax.fori_loop(1, whole, later, 0)
    if z.basis % 16:
        group(whole * 16, z.basis % 16)


def contract(z, mixed, jacobians, first, rows):
    totals = [None] * z.quantities
    for q in range(z.quantities):
        for d in range(3):
            start = 3 * first + d * rows
            if not isinstance(first, int):
                start = pl.multiple_of(start, 16)
            value = mixed[pl.ds(start, rows), q * z.elements : (q + 1) * z.elements]
            for p in range(z.quantities):
                term = value * jacobians[q, p, d : d + 1, :]
                totals[p] = term if totals[p] is None else totals[p] + term
    return totals


def full_rows(value, rows):
    short = rows - value.shape[0]
    if short == 0:
        return value
    return jnp.concatenate([value, jnp.zeros((short, value.shape[1]), value.dtype)], axis=0)


def weight_rows(z, substep, cluster, weights):
    for power, row in enumerate(weights_of(cluster[...], substep)):
        weights[power] = jnp.broadcast_to(row, (8, z.elements))


def predictor_kernel(z, state, jacobians, stiff, weights, moments, rhs, mixed, total):
    e = z.elements
    for q in range(z.quantities):
        for first, rows in z.groups():
            value = state[q, first : first + rows, :]
            total[q, first : first + rows, :] = value * weights[0, 0:1, :]
            put_halves(rhs, z.padded, first, q * e, full_rows(value, 16))

    def derivative(power, carry):
        mixed[...] = product(stiff[...], rhs[...])
        weight = weights[power]

        def group(first, rows):
            sums = contract(z, mixed, jacobians, first, rows)
            for p in range(z.quantities):
                total[p, pl.ds(first, rows), :] += sums[p] * weight[0:1, :]
                put_halves(rhs, z.padded, first, p * e, full_rows(sums[p], 16))

        by_groups(z, group)
        return carry

    lax.fori_loop(1, DERIVATIVES, derivative, 0)
    for q in range(z.quantities):
        for first, rows in z.groups():
            put_halves(moments, z.padded, first, q * e, full_rows(total[q, first : first + rows, :], 16))


def along_lanes(blocks, wanted, elements):
    face, lane = wanted >> (elements.bit_length() - 1), wanted & (elements - 1)
    result = []
    for rows in zip(*blocks):
        picked = jnp.zeros_like(rows[0])
        for j, row in enumerate(rows):
            shape = row.shape
            taken = jnp.take_along_axis(row, jnp.broadcast_to(lane, shape), axis=1, mode="promise_in_bounds")
            picked = jnp.where(jnp.broadcast_to(face == j, shape), taken, picked)
        result.append(picked)
    return result


def dense_rows(z, target, value):
    for q in range(z.quantities):
        target[q * z.face_basis : q * z.face_basis + z.face_rows, :] = value[q * z.face_rows : (q + 1) * z.face_rows]


def send_kernel(z, moments, project, send_hot, send_last, *refs):
    count = len(z.plan)
    outgoing = refs[:count]
    table, faces = refs[count:]
    e, r, half = z.elements, z.face_rows, z.block_padded
    projected = product(project[...], moments[...])
    faces[...] = projected
    blocks = []
    for j in range(z.faces):
        pieces = [projected[j * r : (j + 1) * r, q * e : (q + 1) * e] for q in range(z.quantities)]
        blocks.append([piece[k : k + 8] for piece in pieces for k in range(0, r, 8)])
        high, low = halves(full_rows(jnp.concatenate(pieces, axis=0), half))
        table[:half, j * e : (j + 1) * e] = high
        table[half:, j * e : (j + 1) * e] = low
    by_product = z.by_product
    if by_product:
        picked = product(table[...], send_hot[...])
        for t in range(by_product):
            columns = slice(t * z.slots, (t + 1) * z.slots)
            dense_rows(z, outgoing[t], picked[: z.block, columns] + picked[half : half + z.block, columns])
    for t in range(by_product, count):
        rows = along_lanes(blocks, send_last[t - by_product : t - by_product + 1, :], e)
        dense_rows(z, outgoing[t], jnp.concatenate(rows, axis=0))


def first_kernel(z, *refs):
    given = refs[:8]
    state, jacobians, cluster, turns, stiff, project, send_hot, send_last, weights = refs[8:17]
    wide_stiff, wide_project, stiffness, projection, lists, sizes, arrived = refs[17:]
    targets = [state, jacobians, stiffness, projection, cluster, turns, lists, sizes]
    copies = [pltpu.make_async_copy(given[n], targets[n], arrived.at[n]) for n in range(8)]
    for n in (6, 7, 2, 3, 4, 5, 0, 1):
        copies[n].start()
    for n in (6, 7):
        copies[n].wait()
    slot = lax.broadcasted_iota(jnp.int32, (1, z.slots), 1)
    for t, entry in enumerate(z.plan):
        chosen = lists_of(entry)[0]
        wanted = jnp.where(slot < sizes[0, chosen], lists[pl.ds(chosen, 1), :], -1)
        if t < z.by_product:
            send_hot[:, t * z.slots : (t + 1) * z.slots] = one_hot((z.face_total, z.slots), wanted, 0)
        else:
            send_last[t - z.by_product : t - z.by_product + 1, :] = wanted
    for n in (2, 3, 4):
        copies[n].wait()
    weight_rows(z, 0, cluster, weights)
    stiff[...] = left_parts(wide_stiff, stiffness_rows(z, stiffness, -1.0), z.padded)
    project[...] = left_parts(
        wide_project, [(j * z.face_rows, 0, projection[:, j, :]) for j in range(z.faces)], z.padded
    )
    for n in (5, 0, 1):
        copies[n].wait()


def tables_kernel(z, *refs):
    volume, lift, rotation, neighbours, orient = refs[:5]
    volume_left, lift_left, turned_left, picks, own_hot, far_hot, last_hot = refs[5:12]
    wide_volume, wide_lift, wide_turned = refs[12:]
    e, r, f = z.elements, z.face_rows, z.face_basis
    volume_left[...] = left_parts(wide_volume, stiffness_rows(z, volume, 1.0), z.padded)
    plain, turned = [], []
    for i in range(z.faces):
        face = jnp.transpose(lift[:, i, :], (1, 0))
        plain.append((0, i * r, face))
        for o in range(z.rotations):
            value = jnp.dot(face, rotation[o], precision=lax.Precision.HIGHEST, preferred_element_type=F32)
            turned.append((0, o * z.lifted + i * r, value))
    lift_left[...] = left_parts(wide_lift, plain, z.lifted)
    wide_turned[...] = jnp.zeros_like(wide_turned)
    for row, column, value in turned:
        high = value.astype(BF16).astype(F32)
        columns = slice(column, column + value.shape[1])
        wide_turned[: z.basis, columns] = high
        wide_turned[z.basis :, columns] = value - high
    turned_left[...] = wide_turned[...].astype(BF16)
    for o in range(z.rotations):
        rows = [
            jnp.broadcast_to(jnp.where(orient[i : i + 1, :] == o, 1.0, 0.0), (r, e)) for i in range(z.faces)
        ]
        picks[o] = jnp.concatenate(rows, axis=0).astype(BF16)
    for i in range(z.faces):
        wanted = neighbours[i : i + 1, :]
        own_hot[:, i * e : (i + 1) * e] = one_hot((z.face_total, e), wanted, 0)
        for t, entry in enumerate(z.plan):
            _, direction, exists = lists_of(entry)
            offset = jnp.where(exists, z.face_total + direction * z.slots, -z.slots)
            hot = one_hot((z.slots, e), wanted, offset)
            if t >= z.early:
                row = (t - z.early) * z.slots
                last_hot[row : row + z.slots, i * e : (i + 1) * e] = hot
            else:
                far_hot[t * z.slots : (t + 1) * z.slots, i * e : (i + 1) * e] = hot


def solve(z, index, block, solver, store):
    together = 2 if z.faces % 2 == 0 else 1
    for i in range(0, z.faces, together):
        sums = [[None] * together for _ in range(z.chunk)]
        for q in range(z.quantities):
            for j in range(together):
                value = block(q, i + j)
                for c in range(z.chunk):
                    term = value * solver[q, index * z.chunk + c, i + j : i + j + 1, :]
                    sums[c][j] = term if sums[c][j] is None else sums[c][j] + term
        for c in range(z.chunk):
            column = (index * z.chunk + c) * z.elements
            if not isinstance(column, int):
                column = pl.multiple_of(column, z.elements)
            store(i, together, column, sums[c])


def inner_kernel(z, running, table, faces, moments, jacobians, local_solver, volume_left, lift_left, own_hot, gathered, partial, mixed, rhs):
    e, r = z.elements, z.face_rows
    picked = product(table[...], own_hot[...])
    gathered[...] = picked[: z.block, :] + picked[z.block_padded : z.block_padded + z.block, :]
    def store(i, j, p, values):
        put_halves(rhs, z.lifted, i * r, p, jnp.concatenate(values, axis=0))

    def some(index, carry):
        solve(z, index, lambda q, i: faces[i * r : (i + 1) * r, q * e : (q + 1) * e], local_solver, store)
        return carry

    lax.fori_loop(0, z.quantities // z.chunk, some, 0)
    lifted = product(lift_left[...], rhs[...])
    for q in range(z.quantities):
        partial[q] = running[q] - lifted[:, q * e : (q + 1) * e]
    mixed[...] = product(volume_left[...], moments[...])

    def group(first, rows):
        sums = contract(z, mixed, jacobians, first, rows)
        for p in range(z.quantities):
            partial[p, pl.ds(first, rows), :] += sums[p]

    by_groups(z, group)


def received_blocks(z, incoming, gathered, far_hot, received):
    b, half = z.block, z.block_padded
    for t, source in enumerate(incoming):
        pieces = [source[q * z.face_basis : q * z.face_basis + z.face_rows, :] for q in range(z.quantities)]
        high, low = halves(full_rows(jnp.concatenate(pieces, axis=0), half))
        received[:half, t * z.slots : (t + 1) * z.slots] = high
        received[half:, t * z.slots : (t + 1) * z.slots] = low
    picked = product(received[...], far_hot[...])
    return gathered[...] + picked[:b, :] + picked[half : half + b, :]


def early_kernel(z, *refs):
    *incoming, gathered, far_hot, blocks, received = refs
    blocks[...] = received_blocks(z, incoming, gathered, far_hot, received)


def neighbour_flux(z, incoming, gathered, neighbour_solver, picks, far_hot, turned_left, received, blocks, turned, take):
    e, r, b = z.elements, z.face_rows, z.basis
    blocks[...] = received_blocks(z, incoming, gathered, far_hot, received)
    width = z.rotations * z.lifted

    def store(i, together, column, values):
        high, low = halves(jnp.concatenate(values, axis=0))
        rows = together * r
        for o in range(z.rotations):
            pick = picks[o, i * r : i * r + rows, :]
            row = o * z.lifted + i * r
            turned[row : row + rows, pl.ds(column, e)] = high * pick
            turned[width + row : width + row + rows, pl.ds(column, e)] = low * pick

    for index in range(z.quantities // z.chunk):
        solve(z, index, lambda q, i: blocks[q * r : (q + 1) * r, i * e : (i + 1) * e], neighbour_solver, store)
    both = product(turned_left[...], turned[:width, :])
    flux = both[:b, :] + both[b:, :] + product(turned_left[:b, :], turned[width:, :])
    for q in range(z.quantities):
        take(q, flux[:, q * e : (q + 1) * e])


def flux_kernel(z, substep, *refs):
    incoming, refs = refs[: z.late], refs[z.late :]
    gathered, partial, solution, neighbour_solver, picks, far_hot, turned_left, cluster = refs[:8]
    updated, running, weights, received, blocks, turned = refs[8:]
    weight_rows(z, substep + 1, cluster, weights)
    ending = ((substep + 1) & (period_of(cluster[...]) - 1)) == 0

    def take(q, flux):
        value = partial[q] - flux
        running[q] = value
        updated[q] = jnp.where(ending, value, solution[q])

    neighbour_flux(
        z, incoming, gathered, neighbour_solver, picks, far_hot, turned_left, received, blocks, turned, take
    )


def last_kernel(z, *refs):
    incoming, refs = refs[: z.late], refs[z.late :]
    gathered, partial, neighbour_solver, picks, far_hot, turned_left = refs[:6]
    advanced, received, blocks, turned, done, sent = refs[6:]
    groups = z.quantities // z.chunk

    def copy(index):
        part = pl.ds(index * z.chunk, z.chunk)
        return pltpu.make_async_copy(done.at[part], advanced.at[part], sent.at[index])

    def take(q, flux):
        done[q] = partial[q] - flux

    neighbour_flux(
        z, incoming, gathered, neighbour_solver, picks, far_hot, turned_left, received, blocks, turned, take
    )
    for index in range(groups):
        copy(index).start()
    for index in range(groups):
        copy(index).wait()


def call(body, outs, scratch, cost, arguments, space=pltpu.VMEM, out_space=pltpu.VMEM, more=(), flags=None):
    in_specs = [pl.BlockSpec(memory_space=space)] * len(arguments)
    return pl.pallas_call(
        body,
        out_shape=[jax.ShapeDtypeStruct(shape, kind) for shape, kind in outs],
        in_specs=in_specs,
        out_specs=[pl.BlockSpec(memory_space=out_space)] * len(outs),
        scratch_shapes=[*(pltpu.VMEM(shape, kind) for shape, kind in scratch), *more],
        cost_estimate=pl.CostEstimate(flops=cost, bytes_accessed=1 << 20, transcendentals=0),
        compiler_params=pltpu.CompilerParams(vmem_limit_bytes=24 << 20, flags=flags or {}),
    )(*arguments)


def local(
    plan,
    solution,
    jacobians,
    derivative_stiffness,
    volume_stiffness,
    face_project,
    face_lift,
    face_rotation,
    local_solver,
    neighbour_solver,
    cluster,
    neighbours,
    orient,
    send_faces,
    counts,
):
    z = Sizes(solution, face_project, send_faces, plan)
    count = len(plan)
    sizes = [lax.axis_size(axis) for axis in AXES]
    state = solution.transpose(1, 0, 2)
    jacobians = jacobians.transpose(1, 2, 0, 3)
    local_solver = local_solver.transpose(1, 2, 0, 3)
    neighbour_solver = neighbour_solver.transpose(1, 2, 0, 3)
    projection = face_project.transpose(1, 0, 2)
    lift = face_lift.transpose(2, 0, 1)
    cluster = cluster.reshape(1, -1)
    counts = counts.reshape(1, -1)

    block = (((z.quantities - 1) * z.face_basis + z.face_rows, z.slots), F32)
    table = ((2 * z.block_padded, z.face_total), BF16)
    faces = ((z.lifted, z.columns), F32)
    moments = ((3 * z.padded, z.columns), BF16)
    stiff = ((3 * z.basis, 3 * z.padded), BF16)
    project = ((z.lifted, 3 * z.padded), BF16)
    field = ((z.quantities, z.basis, z.elements), F32)
    gathered = ((z.block, z.face_total), F32)
    send_hot = ((z.face_total, max(1, z.by_product) * z.slots), BF16)
    send_last = ((max(1, count - z.by_product), z.slots), jnp.int32)
    far_hot = ((z.early * z.slots, z.face_total), BF16)
    last_hot = ((z.late * z.slots, z.face_total), BF16)
    own_hot = ((z.face_total, z.face_total), BF16)
    lift_left = ((z.basis, 3 * z.lifted), BF16)
    turned_left = ((2 * z.basis, z.rotations * z.lifted), BF16)
    picks = ((z.rotations, z.lifted, z.elements), BF16)
    mixed = ((3 * z.basis, z.columns), F32)
    weights = ((DERIVATIVES, 8, z.elements), F32)
    received = ((2 * z.block_padded, z.early * z.slots), BF16)
    last_received = ((2 * z.block_padded, z.late * z.slots), BF16)
    turned = ((2 * z.rotations * z.lifted, z.columns), BF16)

    def wide(entry):
        return (entry[0], F32)

    given = (
        state, jacobians, derivative_stiffness, projection, cluster, face_rotation, send_faces, counts,
    )
    results = call(
        functools.partial(first_kernel, z),
        [(given[n].shape, given[n].dtype) for n in (0, 1, 4, 5)] + [stiff, project, send_hot, send_last, weights],
        [wide(stiff), wide(project)],
        1_000_000,
        tuple(pltpu.with_memory_space_constraint(value, pltpu.HBM) for value in given),
        space=pltpu.HBM,
        more=[
            *(pltpu.VMEM(given[n].shape, given[n].dtype) for n in (2, 3, 6)),
            pltpu.SMEM(counts.shape, counts.dtype),
            pltpu.SemaphoreType.DMA((len(given),)),
        ],
    )
    state, jacobians, cluster, turns, stiff_left, project_left, send_matrix, send_rest, weights_now = results
    running = state
    for substep in range(SUBSTEPS):
        (moments_now,) = call(
            functools.partial(predictor_kernel, z),
            [moments],
            [moments, mixed, field],
            10_000_000,
            (state, jacobians, stiff_left, weights_now),
        )
        *outgoing, table_now, faces_now = call(
            functools.partial(send_kernel, z),
            [block] * count + [table, faces],
            [],
            5_000_000,
            (moments_now, project_left, send_matrix, send_rest),
        )
        incoming = [lax.ppermute(value, AXES, partners(sizes, entry)) for value, entry in zip(outgoing, plan)]
        if substep == 0:
            volume_left, lift_plain, lift_turned, orient_picks, own_matrix, far_matrix, last_matrix = call(
                functools.partial(tables_kernel, z),
                [stiff, lift_left, turned_left, picks, own_hot, far_hot, last_hot],
                [wide(stiff), wide(lift_left), wide(turned_left)],
                1_000_000,
                (volume_stiffness, lift, turns, neighbours, orient),
            )
        gathered_now, partial = call(
            functools.partial(inner_kernel, z),
            [gathered, field],
            [mixed, ((3 * z.lifted, z.columns), BF16)],
            10_000_000,
            (running, table_now, faces_now, moments_now, jacobians, local_solver, volume_left, lift_plain, own_matrix),
        )
        (gathered_now,) = call(
            functools.partial(early_kernel, z),
            [gathered],
            [received],
            5_000_000,
            (*incoming[: z.early], gathered_now, far_matrix),
        )
        if substep == SUBSTEPS - 1:
            (advanced,) = call(
                functools.partial(last_kernel, z),
                [field],
                [last_received, gathered, turned, field],
                10_000_000,
                (*incoming[z.early :], gathered_now, partial, neighbour_solver, orient_picks, last_matrix, lift_turned),
                out_space=pltpu.HBM,
                more=[pltpu.SemaphoreType.DMA((z.quantities // z.chunk,))],
            )
            return advanced.transpose(1, 0, 2)
        state, running, weights_now = call(
            functools.partial(flux_kernel, z, substep),
            [field, field, weights],
            [last_received, gathered, turned],
            10_000_000,
            (
                *incoming[z.early :], gathered_now, partial, state, neighbour_solver, orient_picks, last_matrix, lift_turned,
                cluster,
            ),
        )


def solution(mesh):
    spread = ("gx", "gy", "gz")
    return jax.shard_map(
        functools.partial(local, exchange_plan(mesh)),
        mesh=mesh,
        in_specs=(
            P(None, None, spread),
            P(None, None, None, spread),
            P(),
            P(),
            P(),
            P(),
            P(),
            P(None, None, None, spread),
            P(None, None, None, spread),
            P(spread),
            P(None, spread),
            P(None, spread),
            P(None, spread),
            P(None, spread),
        ),
        out_specs=P(None, None, spread),
        check_vma=False,
    )
```

```python
import functools
import math

import jax
import jax.numpy as jnp
from jax import lax
from jax.experimental import pallas as pl
from jax.experimental.pallas import tpu as pltpu
from jax.sharding import PartitionSpec as P

DERIVATIVES = 6
SUBSTEPS = 4
SPAN = 1.0
F32 = jnp.float32
BF16 = jnp.bfloat16
AXES = ("gx", "gy", "gz")


def rounded(size, unit):
    return -(-size // unit) * unit


def halves(value):
    high = value.astype(BF16)
    return high, (value - high.astype(F32)).astype(BF16)


def product(left, right):
    return jnp.dot(left, right, preferred_element_type=F32)


def exchange_plan(mesh):
    plan = []
    for number, axis in enumerate(AXES):
        size = mesh.shape[axis]
        if size == 1:
            continue
        if size == 2:
            plan.append((number, size, "pair0"))
        elif size % 2 == 0:
            plan.append((number, size, "pair0"))
            plan.append((number, size, "pair1"))
        else:
            plan.append((number, size, "up"))
            plan.append((number, size, "down"))
    return tuple(sorted(plan, key=lambda entry: (entry[2] == "pair1", entry[0] != 2)))


def partners(sizes, entry):
    number, size, kind = entry
    spare = [other for other in (2, 0, 1) if other != number and sizes[other] % 2 == 0]
    pairs = []
    for flat in range(math.prod(sizes)):
        place = [flat // (sizes[1] * sizes[2]), flat // sizes[2] % sizes[1], flat % sizes[2]]
        source = flat
        here = place[number]
        if kind in ("up", "down"):
            place[number] = (here + (1 if kind == "up" else -1)) % size
        elif kind == "pair0":
            place[number] = here ^ 1
        elif 0 < here < size - 1:
            place[number] = ((here + 1) ^ 1) - 1
        elif spare:
            place[spare[0]] ^= 1
        else:
            place[number] = size - 1 - here
        pairs.append((source, (place[0] * sizes[1] + place[1]) * sizes[2] + place[2]))
    return pairs


def lists_of(entry):
    number, size, kind = entry
    place = lax.axis_index(AXES[number])
    if kind == "up":
        return 2 * number, 2 * number, place > 0
    if kind == "down":
        return 2 * number + 1, 2 * number + 1, place < size - 1
    parity = lax.rem(place, 2)
    upper = parity if kind == "pair0" else 1 - parity
    exists = jnp.where(upper == 1, place > 0, place < size - 1)
    return 2 * number + upper, 2 * number + 1 - upper, exists


class Sizes:
    def __init__(self, solution, face_project, send_faces, plan):
        self.basis, self.quantities, self.elements = solution.shape
        self.faces, self.face_basis, _ = face_project.shape
        self.slots = send_faces.shape[1]
        self.plan = plan
        self.padded = rounded(self.basis, 16)
        self.face_rows = rounded(self.face_basis, 8)
        self.block = self.quantities * self.face_rows
        self.block_padded = rounded(self.block, 16)
        self.columns = self.quantities * self.elements
        self.face_total = self.faces * self.elements
        self.lifted = self.faces * self.face_rows
        self.rotations = 3
        count = len(plan)
        self.by_product = count - 1 if count % 2 and count > 1 and self.elements == 128 else count
        self.late = min(2, count - 1) if count > 1 else 0
        self.early = count - self.late
        self.chunk = 3 if self.quantities % 3 == 0 else 1

    def groups(self):
        return [(k, min(16, self.basis - k)) for k in range(0, self.basis, 16)]


def left_parts(scratch, pieces, width):
    scratch[...] = jnp.zeros_like(scratch)
    for row, column, value in pieces:
        high = value.astype(BF16).astype(F32)
        rows, columns = value.shape
        scratch[row : row + rows, column : column + columns] = high
        scratch[row : row + rows, width + column : width + column + columns] = high
        scratch[row : row + rows, 2 * width + column : 2 * width + column + columns] = value - high
    return scratch[...].astype(BF16)


def stiffness_rows(z, matrices, sign):
    pieces = []
    for first, rows in z.groups():
        for d in range(3):
            pieces.append((3 * first + d * rows, 0, sign * matrices[d, first : first + rows, :]))
    return pieces


def one_hot(shape, targets, offset):
    rows = lax.broadcasted_iota(jnp.int32, shape, 0)
    return jnp.where(rows == targets - offset, 1.0, 0.0).astype(BF16)


def period_of(cluster):
    return jnp.left_shift(jnp.ones_like(cluster), cluster)


def weights_of(cluster, substep):
    offset = (substep & (period_of(cluster) - 1)).astype(F32)
    step = SPAN / SUBSTEPS
    upper, lower = (offset + 1.0) * step, offset * step
    rows, high, low = [], upper, lower
    for power in range(DERIVATIVES):
        rows.append((high - low) * (1.0 / math.factorial(power + 1)))
        high, low = high * upper, low * lower
    return rows


def put_halves(target, width, row, column, value):
    high, low = halves(value)
    rows, columns = value.shape
    for part, piece in enumerate((high, low, high)):
        start = part * width + row
        if not isinstance(row, int):
            start = pl.multiple_of(start, 16)
        target[pl.ds(start, rows), pl.ds(column, columns)] = piece


def by_groups(z, group):
    whole = z.basis // 16
    group(0, 16)

    def later(index, carry):
        group(pl.multiple_of(index * 16, 16), 16)
        return carry

    lax.fori_loop(1, whole, later, 0)
    if z.basis % 16:
        group(whole * 16, z.basis % 16)


def contract(z, mixed, jacobians, first, rows):
    totals = [None] * z.quantities
    for q in range(z.quantities):
        for d in range(3):
            start = 3 * first + d * rows
            if not isinstance(first, int):
                start = pl.multiple_of(start, 16)
            value = mixed[pl.ds(start, rows), q * z.elements : (q + 1) * z.elements]
            for p in range(z.quantities):
                term = value * jacobians[q, p, d : d + 1, :]
                totals[p] = term if totals[p] is None else totals[p] + term
    return totals


def full_rows(value, rows):
    short = rows - value.shape[0]
    if short == 0:
        return value
    return jnp.concatenate([value, jnp.zeros((short, value.shape[1]), value.dtype)], axis=0)


def weight_rows(z, substep, cluster, weights):
    for power, row in enumerate(weights_of(cluster[...], substep)):
        weights[power] = jnp.broadcast_to(row, (8, z.elements))


def predictor_kernel(z, state, jacobians, stiff, weights, moments, rhs, mixed, total):
    e = z.elements
    for q in range(z.quantities):
        for first, rows in z.groups():
            value = state[q, first : first + rows, :]
            total[q, first : first + rows, :] = value * weights[0, 0:1, :]
            put_halves(rhs, z.padded, first, q * e, full_rows(value, 16))

    def derivative(power, carry):
        mixed[...] = product(stiff[...], rhs[...])
        weight = weights[power]

        def group(first, rows):
            sums = contract(z, mixed, jacobians, first, rows)
            for p in range(z.quantities):
                total[p, pl.ds(first, rows), :] += sums[p] * weight[0:1, :]
                put_halves(rhs, z.padded, first, p * e, full_rows(sums[p], 16))

        by_groups(z, group)
        return carry

    lax.fori_loop(1, DERIVATIVES, derivative, 0)
    for q in range(z.quantities):
        for first, rows in z.groups():
            put_halves(moments, z.padded, first, q * e, full_rows(total[q, first : first + rows, :], 16))


def along_lanes(blocks, wanted, elements):
    face, lane = wanted >> (elements.bit_length() - 1), wanted & (elements - 1)
    result = []
    for rows in zip(*blocks):
        picked = jnp.zeros_like(rows[0])
        for j, row in enumerate(rows):
            shape = row.shape
            taken = jnp.take_along_axis(row, jnp.broadcast_to(lane, shape), axis=1, mode="promise_in_bounds")
            picked = jnp.where(jnp.broadcast_to(face == j, shape), taken, picked)
        result.append(picked)
    return result


def dense_rows(z, target, value):
    for q in range(z.quantities):
        target[q * z.face_basis : q * z.face_basis + z.face_rows, :] = value[q * z.face_rows : (q + 1) * z.face_rows]


def send_kernel(z, moments, project, send_hot, send_last, *refs):
    count = len(z.plan)
    outgoing = refs[:count]
    table, faces = refs[count:]
    e, r, half = z.elements, z.face_rows, z.block_padded
    projected = product(project[...], moments[...])
    faces[...] = projected
    blocks = []
    for j in range(z.faces):
        pieces = [projected[j * r : (j + 1) * r, q * e : (q + 1) * e] for q in range(z.quantities)]
        blocks.append([piece[k : k + 8] for piece in pieces for k in range(0, r, 8)])
        high, low = halves(full_rows(jnp.concatenate(pieces, axis=0), half))
        table[:half, j * e : (j + 1) * e] = high
        table[half:, j * e : (j + 1) * e] = low
    by_product = z.by_product
    if by_product:
        picked = product(table[...], send_hot[...])
        for t in range(by_product):
            columns = slice(t * z.slots, (t + 1) * z.slots)
            dense_rows(z, outgoing[t], picked[: z.block, columns] + picked[half : half + z.block, columns])
    for t in range(by_product, count):
        rows = along_lanes(blocks, send_last[t - by_product : t - by_product + 1, :], e)
        dense_rows(z, outgoing[t], jnp.concatenate(rows, axis=0))


def first_kernel(z, *refs):
    given = refs[:8]
    state, jacobians, cluster, turns, stiff, project, send_hot, send_last, weights = refs[8:17]
    wide_stiff, wide_project, stiffness, projection, lists, sizes, arrived = refs[17:]
    targets = [state, jacobians, stiffness, projection, cluster, turns, lists, sizes]
    copies = [pltpu.make_async_copy(given[n], targets[n], arrived.at[n]) for n in range(8)]
    for n in (6, 7, 2, 3, 4, 5, 0, 1):
        copies[n].start()
    for n in (6, 7):
        copies[n].wait()
    slot = lax.broadcasted_iota(jnp.int32, (1, z.slots), 1)
    for t, entry in enumerate(z.plan):
        chosen = lists_of(entry)[0]
        wanted = jnp.where(slot < sizes[0, chosen], lists[pl.ds(chosen, 1), :], -1)
        if t < z.by_product:
            send_hot[:, t * z.slots : (t + 1) * z.slots] = one_hot((z.face_total, z.slots), wanted, 0)
        else:
            send_last[t - z.by_product : t - z.by_product + 1, :] = wanted
    for n in (2, 3, 4):
        copies[n].wait()
    weight_rows(z, 0, cluster, weights)
    stiff[...] = left_parts(wide_stiff, stiffness_rows(z, stiffness, -1.0), z.padded)
    project[...] = left_parts(
        wide_project, [(j * z.face_rows, 0, projection[:, j, :]) for j in range(z.faces)], z.padded
    )
    for n in (5, 0, 1):
        copies[n].wait()


def tables_kernel(z, *refs):
    volume, lift, rotation, neighbours, orient = refs[:5]
    volume_left, lift_left, turned_left, picks, own_hot, far_hot, last_hot = refs[5:12]
    wide_volume, wide_lift, wide_turned = refs[12:]
    e, r, f = z.elements, z.face_rows, z.face_basis
    volume_left[...] = left_parts(wide_volume, stiffness_rows(z, volume, 1.0), z.padded)
    plain, turned = [], []
    for i in range(z.faces):
        face = jnp.transpose(lift[:, i, :], (1, 0))
        plain.append((0, i * r, face))
        for o in range(z.rotations):
            value = jnp.dot(face, rotation[o], precision=lax.Precision.HIGHEST, preferred_element_type=F32)
            turned.append((0, o * z.lifted + i * r, value))
    lift_left[...] = left_parts(wide_lift, plain, z.lifted)
    wide_turned[...] = jnp.zeros_like(wide_turned)
    for row, column, value in turned:
        high = value.astype(BF16).astype(F32)
        columns = slice(column, column + value.shape[1])
        wide_turned[: z.basis, columns] = high
        wide_turned[z.basis :, columns] = value - high
    turned_left[...] = wide_turned[...].astype(BF16)
    for o in range(z.rotations):
        rows = [
            jnp.broadcast_to(jnp.where(orient[i : i + 1, :] == o, 1.0, 0.0), (r, e)) for i in range(z.faces)
        ]
        picks[o] = jnp.concatenate(rows, axis=0).astype(BF16)
    for i in range(z.faces):
        wanted = neighbours[i : i + 1, :]
        own_hot[:, i * e : (i + 1) * e] = one_hot((z.face_total, e), wanted, 0)
        for t, entry in enumerate(z.plan):
            _, direction, exists = lists_of(entry)
            offset = jnp.where(exists, z.face_total + direction * z.slots, -z.slots)
            hot = one_hot((z.slots, e), wanted, offset)
            if t >= z.early:
                row = (t - z.early) * z.slots
                last_hot[row : row + z.slots, i * e : (i + 1) * e] = hot
            else:
                far_hot[t * z.slots : (t + 1) * z.slots, i * e : (i + 1) * e] = hot


def solve(z, index, block, solver, store):
    together = 2 if z.faces % 2 == 0 else 1
    for i in range(0, z.faces, together):
        sums = [[None] * together for _ in range(z.chunk)]
        for q in range(z.quantities):
            for j in range(together):
                value = block(q, i + j)
                for c in range(z.chunk):
                    term = value * solver[q, index * z.chunk + c, i + j : i + j + 1, :]
                    sums[c][j] = term if sums[c][j] is None else sums[c][j] + term
        for c in range(z.chunk):
            column = (index * z.chunk + c) * z.elements
            if not isinstance(column, int):
                column = pl.multiple_of(column, z.elements)
            store(i, together, column, sums[c])


def inner_kernel(z, running, table, faces, moments, jacobians, local_solver, volume_left, lift_left, own_hot, gathered, partial, mixed, rhs):
    e, r = z.elements, z.face_rows
    picked = product(table[...], own_hot[...])
    gathered[...] = picked[: z.block, :] + picked[z.block_padded : z.block_padded + z.block, :]
    def store(i, j, p, values):
        put_halves(rhs, z.lifted, i * r, p, jnp.concatenate(values, axis=0))

    def some(index, carry):
        solve(z, index, lambda q, i: faces[i * r : (i + 1) * r, q * e : (q + 1) * e], local_solver, store)
        return carry

    lax.fori_loop(0, z.quantities // z.chunk, some, 0)
    lifted = product(lift_left[...], rhs[...])
    for q in range(z.quantities):
        partial[q] = running[q] - lifted[:, q * e : (q + 1) * e]
    mixed[...] = product(volume_left[...], moments[...])

    def group(first, rows):
        sums = contract(z, mixed, jacobians, first, rows)
        for p in range(z.quantities):
            partial[p, pl.ds(first, rows), :] += sums[p]

    by_groups(z, group)


def received_blocks(z, incoming, gathered, far_hot, received):
    b, half = z.block, z.block_padded
    for t, source in enumerate(incoming):
        pieces = [source[q * z.face_basis : q * z.face_basis + z.face_rows, :] for q in range(z.quantities)]
        high, low = halves(full_rows(jnp.concatenate(pieces, axis=0), half))
        received[:half, t * z.slots : (t + 1) * z.slots] = high
        received[half:, t * z.slots : (t + 1) * z.slots] = low
    picked = product(received[...], far_hot[...])
    return gathered[...] + picked[:b, :] + picked[half : half + b, :]


def early_kernel(z, *refs):
    *incoming, gathered, far_hot, blocks, received = refs
    blocks[...] = received_blocks(z, incoming, gathered, far_hot, received)


def neighbour_flux(z, incoming, gathered, neighbour_solver, picks, far_hot, turned_left, received, blocks, turned, take):
    e, r, b = z.elements, z.face_rows, z.basis
    blocks[...] = received_blocks(z, incoming, gathered, far_hot, received)
    width = z.rotations * z.lifted

    def store(i, together, column, values):
        high, low = halves(jnp.concatenate(values, axis=0))
        rows = together * r
        for o in range(z.rotations):
            pick = picks[o, i * r : i * r + rows, :]
            row = o * z.lifted + i * r
            turned[row : row + rows, pl.ds(column, e)] = high * pick
            turned[width + row : width + row + rows, pl.ds(column, e)] = low * pick

    for index in range(z.quantities // z.chunk):
        solve(z, index, lambda q, i: blocks[q * r : (q + 1) * r, i * e : (i + 1) * e], neighbour_solver, store)
    both = product(turned_left[...], turned[:width, :])
    flux = both[:b, :] + both[b:, :] + product(turned_left[:b, :], turned[width:, :])
    for q in range(z.quantities):
        take(q, flux[:, q * e : (q + 1) * e])


def flux_kernel(z, substep, *refs):
    incoming, refs = refs[: z.late], refs[z.late :]
    gathered, partial, solution, neighbour_solver, picks, far_hot, turned_left, cluster = refs[:8]
    updated, running, weights, received, blocks, turned = refs[8:]
    weight_rows(z, substep + 1, cluster, weights)
    ending = ((substep + 1) & (period_of(cluster[...]) - 1)) == 0

    def take(q, flux):
        value = partial[q] - flux
        running[q] = value
        updated[q] = jnp.where(ending, value, solution[q])

    neighbour_flux(
        z, incoming, gathered, neighbour_solver, picks, far_hot, turned_left, received, blocks, turned, take
    )


def last_kernel(z, *refs):
    incoming, refs = refs[: z.late], refs[z.late :]
    gathered, partial, neighbour_solver, picks, far_hot, turned_left = refs[:6]
    advanced, received, blocks, turned, done, sent = refs[6:]
    groups = z.quantities // z.chunk

    def copy(index):
        part = pl.ds(index * z.chunk, z.chunk)
        return pltpu.make_async_copy(done.at[part], advanced.at[part], sent.at[index])

    def take(q, flux):
        done[q] = partial[q] - flux

    neighbour_flux(
        z, incoming, gathered, neighbour_solver, picks, far_hot, turned_left, received, blocks, turned, take
    )
    for index in range(groups):
        copy(index).start()
    for index in range(groups):
        copy(index).wait()


def call(body, outs, scratch, cost, arguments, space=pltpu.VMEM, out_space=pltpu.VMEM, more=(), flags=None):
    in_specs = [pl.BlockSpec(memory_space=space)] * len(arguments)
    return pl.pallas_call(
        body,
        out_shape=[jax.ShapeDtypeStruct(shape, kind) for shape, kind in outs],
        in_specs=in_specs,
        out_specs=[pl.BlockSpec(memory_space=out_space)] * len(outs),
        scratch_shapes=[*(pltpu.VMEM(shape, kind) for shape, kind in scratch), *more],
        cost_estimate=pl.CostEstimate(flops=cost, bytes_accessed=1 << 20, transcendentals=0),
        compiler_params=pltpu.CompilerParams(vmem_limit_bytes=24 << 20, flags=flags or {}),
    )(*arguments)


def local(
    plan,
    solution,
    jacobians,
    derivative_stiffness,
    volume_stiffness,
    face_project,
    face_lift,
    face_rotation,
    local_solver,
    neighbour_solver,
    cluster,
    neighbours,
    orient,
    send_faces,
    counts,
):
    z = Sizes(solution, face_project, send_faces, plan)
    count = len(plan)
    sizes = [lax.axis_size(axis) for axis in AXES]
    state = solution.transpose(1, 0, 2)
    jacobians = jacobians.transpose(1, 2, 0, 3)
    local_solver = local_solver.transpose(1, 2, 0, 3)
    neighbour_solver = neighbour_solver.transpose(1, 2, 0, 3)
    projection = face_project.transpose(1, 0, 2)
    lift = face_lift.transpose(2, 0, 1)
    cluster = cluster.reshape(1, -1)
    counts = counts.reshape(1, -1)

    block = (((z.quantities - 1) * z.face_basis + z.face_rows, z.slots), F32)
    table = ((2 * z.block_padded, z.face_total), BF16)
    faces = ((z.lifted, z.columns), F32)
    moments = ((3 * z.padded, z.columns), BF16)
    stiff = ((3 * z.basis, 3 * z.padded), BF16)
    project = ((z.lifted, 3 * z.padded), BF16)
    field = ((z.quantities, z.basis, z.elements), F32)
    gathered = ((z.block, z.face_total), F32)
    send_hot = ((z.face_total, max(1, z.by_product) * z.slots), BF16)
    send_last = ((max(1, count - z.by_product), z.slots), jnp.int32)
    far_hot = ((z.early * z.slots, z.face_total), BF16)
    last_hot = ((z.late * z.slots, z.face_total), BF16)
    own_hot = ((z.face_total, z.face_total), BF16)
    lift_left = ((z.basis, 3 * z.lifted), BF16)
    turned_left = ((2 * z.basis, z.rotations * z.lifted), BF16)
    picks = ((z.rotations, z.lifted, z.elements), BF16)
    mixed = ((3 * z.basis, z.columns), F32)
    weights = ((DERIVATIVES, 8, z.elements), F32)
    received = ((2 * z.block_padded, z.early * z.slots), BF16)
    last_received = ((2 * z.block_padded, z.late * z.slots), BF16)
    turned = ((2 * z.rotations * z.lifted, z.columns), BF16)

    def wide(entry):
        return (entry[0], F32)

    given = (
        state, jacobians, derivative_stiffness, projection, cluster, face_rotation, send_faces, counts,
    )
    results = call(
        functools.partial(first_kernel, z),
        [(given[n].shape, given[n].dtype) for n in (0, 1, 4, 5)] + [stiff, project, send_hot, send_last, weights],
        [wide(stiff), wide(project)],
        1_000_000,
        tuple(pltpu.with_memory_space_constraint(value, pltpu.HBM) for value in given),
        space=pltpu.HBM,
        more=[
            *(pltpu.VMEM(given[n].shape, given[n].dtype) for n in (2, 3, 6)),
            pltpu.SMEM(counts.shape, counts.dtype),
            pltpu.SemaphoreType.DMA((len(given),)),
        ],
    )
    state, jacobians, cluster, turns, stiff_left, project_left, send_matrix, send_rest, weights_now = results
    running = state
    for substep in range(SUBSTEPS):
        (moments_now,) = call(
            functools.partial(predictor_kernel, z),
            [moments],
            [moments, mixed, field],
            10_000_000,
            (state, jacobians, stiff_left, weights_now),
        )
        *outgoing, table_now, faces_now = call(
            functools.partial(send_kernel, z),
            [block] * count + [table, faces],
            [],
            5_000_000,
            (moments_now, project_left, send_matrix, send_rest),
        )
        incoming = [lax.ppermute(value, AXES, partners(sizes, entry)) for value, entry in zip(outgoing, plan)]
        if substep == 0:
            volume_left, lift_plain, lift_turned, orient_picks, own_matrix, far_matrix, last_matrix = call(
                functools.partial(tables_kernel, z),
                [stiff, lift_left, turned_left, picks, own_hot, far_hot, last_hot],
                [wide(stiff), wide(lift_left), wide(turned_left)],
                1_000_000,
                (volume_stiffness, lift, turns, neighbours, orient),
            )
        gathered_now, partial = call(
            functools.partial(inner_kernel, z),
            [gathered, field],
            [mixed, ((3 * z.lifted, z.columns), BF16)],
            10_000_000,
            (running, table_now, faces_now, moments_now, jacobians, local_solver, volume_left, lift_plain, own_matrix),
        )
        (gathered_now,) = call(
            functools.partial(early_kernel, z),
            [gathered],
            [received],
            5_000_000,
            (*incoming[: z.early], gathered_now, far_matrix),
        )
        if substep == SUBSTEPS - 1:
            (advanced,) = call(
                functools.partial(last_kernel, z),
                [field],
                [last_received, gathered, turned, field],
                10_000_000,
                (*incoming[z.early :], gathered_now, partial, neighbour_solver, orient_picks, last_matrix, lift_turned),
                out_space=pltpu.HBM,
                more=[pltpu.SemaphoreType.DMA((z.quantities // z.chunk,))],
            )
            return advanced.transpose(1, 0, 2)
        state, running, weights_now = call(
            functools.partial(flux_kernel, z, substep),
            [field, field, weights],
            [last_received, gathered, turned],
            10_000_000,
            (
                *incoming[z.early :], gathered_now, partial, state, neighbour_solver, orient_picks, last_matrix, lift_turned,
                cluster,
            ),
        )


def solution(mesh):
    spread = ("gx", "gy", "gz")
    return jax.shard_map(
        functools.partial(local, exchange_plan(mesh)),
        mesh=mesh,
        in_specs=(
            P(None, None, spread),
            P(None, None, None, spread),
            P(),
            P(),
            P(),
            P(),
            P(),
            P(None, None, None, spread),
            P(None, None, None, spread),
            P(spread),
            P(None, spread),
            P(None, spread),
            P(None, spread),
            P(None, spread),
        ),
        out_specs=P(None, None, spread),
        check_vma=False,
    )
```

```python
import functools
import math

import jax
import jax.numpy as jnp
from jax import lax
from jax.experimental import pallas as pl
from jax.experimental.pallas import tpu as pltpu
from jax.sharding import PartitionSpec as P

DERIVATIVES = 6
SUBSTEPS = 4
SPAN = 1.0
F32 = jnp.float32
BF16 = jnp.bfloat16
AXES = ("gx", "gy", "gz")


def rounded(size, unit):
    return -(-size // unit) * unit


def halves(value):
    high = value.astype(BF16)
    return high, (value - high.astype(F32)).astype(BF16)


def product(left, right):
    return jnp.dot(left, right, preferred_element_type=F32)


def exchange_plan(mesh):
    plan = []
    for number, axis in enumerate(AXES):
        size = mesh.shape[axis]
        if size == 1:
            continue
        if size == 2:
            plan.append((number, size, "pair0"))
        elif size % 2 == 0:
            plan.append((number, size, "pair0"))
            plan.append((number, size, "pair1"))
        else:
            plan.append((number, size, "up"))
            plan.append((number, size, "down"))
    return tuple(sorted(plan, key=lambda entry: (entry[2] == "pair1", entry[2] == "pair0" and entry[0] != 2)))


def partners(sizes, entry):
    number, size, kind = entry
    spare = [other for other in (2, 0, 1) if other != number and sizes[other] % 2 == 0]
    pairs = []
    for flat in range(math.prod(sizes)):
        place = [flat // (sizes[1] * sizes[2]), flat // sizes[2] % sizes[1], flat % sizes[2]]
        source = flat
        here = place[number]
        if kind in ("up", "down"):
            place[number] = (here + (1 if kind == "up" else -1)) % size
        elif kind == "pair0":
            place[number] = here ^ 1
        elif 0 < here < size - 1:
            place[number] = ((here + 1) ^ 1) - 1
        elif spare:
            place[spare[0]] ^= 1
        else:
            place[number] = size - 1 - here
        pairs.append((source, (place[0] * sizes[1] + place[1]) * sizes[2] + place[2]))
    return pairs


def lists_of(entry):
    number, size, kind = entry
    place = lax.axis_index(AXES[number])
    if kind == "up":
        return 2 * number, 2 * number, place > 0
    if kind == "down":
        return 2 * number + 1, 2 * number + 1, place < size - 1
    parity = lax.rem(place, 2)
    upper = parity if kind == "pair0" else 1 - parity
    exists = jnp.where(upper == 1, place > 0, place < size - 1)
    return 2 * number + upper, 2 * number + 1 - upper, exists


class Sizes:
    def __init__(self, solution, face_project, send_faces, plan):
        self.basis, self.quantities, self.elements = solution.shape
        self.faces, self.face_basis, _ = face_project.shape
        self.slots = send_faces.shape[1]
        self.plan = plan
        self.padded = rounded(self.basis, 16)
        self.face_rows = rounded(self.face_basis, 8)
        self.block = self.quantities * self.face_rows
        self.block_padded = rounded(self.block, 16)
        self.columns = self.quantities * self.elements
        self.face_total = self.faces * self.elements
        self.lifted = self.faces * self.face_rows
        self.rotations = 3
        count = len(plan)
        self.by_product = count - 1 if count % 2 and count > 1 and self.elements == 128 else count
        self.late = min(2, count - 1) if count > 1 else 0
        self.early = count - self.late
        self.chunk = 3 if self.quantities % 3 == 0 else 1

    def groups(self):
        return [(k, min(16, self.basis - k)) for k in range(0, self.basis, 16)]


def left_parts(scratch, pieces, width):
    scratch[...] = jnp.zeros_like(scratch)
    for row, column, value in pieces:
        high = value.astype(BF16).astype(F32)
        rows, columns = value.shape
        scratch[row : row + rows, column : column + columns] = high
        scratch[row : row + rows, width + column : width + column + columns] = high
        scratch[row : row + rows, 2 * width + column : 2 * width + column + columns] = value - high
    return scratch[...].astype(BF16)


def stiffness_rows(z, matrices, sign):
    pieces = []
    for first, rows in z.groups():
        for d in range(3):
            pieces.append((3 * first + d * rows, 0, sign * matrices[d, first : first + rows, :]))
    return pieces


def one_hot(shape, targets, offset):
    rows = lax.broadcasted_iota(jnp.int32, shape, 0)
    return jnp.where(rows == targets - offset, 1.0, 0.0).astype(BF16)


def period_of(cluster):
    return jnp.left_shift(jnp.ones_like(cluster), cluster)


def weights_of(cluster, substep):
    offset = (substep & (period_of(cluster) - 1)).astype(F32)
    step = SPAN / SUBSTEPS
    upper, lower = (offset + 1.0) * step, offset * step
    rows, high, low = [], upper, lower
    for power in range(DERIVATIVES):
        rows.append((high - low) * (1.0 / math.factorial(power + 1)))
        high, low = high * upper, low * lower
    return rows


def put_halves(target, width, row, column, value):
    high, low = halves(value)
    rows, columns = value.shape
    for part, piece in enumerate((high, low, high)):
        start = part * width + row
        if not isinstance(row, int):
            start = pl.multiple_of(start, 16)
        target[pl.ds(start, rows), pl.ds(column, columns)] = piece


def by_groups(z, group):
    whole = z.basis // 16
    group(0, 16)

    def later(index, carry):
        group(pl.multiple_of(index * 16, 16), 16)
        return carry

    lax.fori_loop(1, whole, later, 0)
    if z.basis % 16:
        group(whole * 16, z.basis % 16)


def contract(z, mixed, jacobians, first, rows):
    totals = [None] * z.quantities
    for q in range(z.quantities):
        for d in range(3):
            start = 3 * first + d * rows
            if not isinstance(first, int):
                start = pl.multiple_of(start, 16)
            value = mixed[pl.ds(start, rows), q * z.elements : (q + 1) * z.elements]
            for p in range(z.quantities):
                term = value * jacobians[q, p, d : d + 1, :]
                totals[p] = term if totals[p] is None else totals[p] + term
    return totals


def full_rows(value, rows):
    short = rows - value.shape[0]
    if short == 0:
        return value
    return jnp.concatenate([value, jnp.zeros((short, value.shape[1]), value.dtype)], axis=0)


def weight_rows(z, substep, cluster, weights):
    for power, row in enumerate(weights_of(cluster[...], substep)):
        weights[power] = jnp.broadcast_to(row, (8, z.elements))


def predictor_kernel(z, state, jacobians, stiff, weights, moments, rhs, mixed, total):
    e = z.elements
    for q in range(z.quantities):
        for first, rows in z.groups():
            value = state[q, first : first + rows, :]
            total[q, first : first + rows, :] = value * weights[0, 0:1, :]
            put_halves(rhs, z.padded, first, q * e, full_rows(value, 16))

    def derivative(power, carry):
        mixed[...] = product(stiff[...], rhs[...])
        weight = weights[power]

        def group(first, rows):
            sums = contract(z, mixed, jacobians, first, rows)
            for p in range(z.quantities):
                total[p, pl.ds(first, rows), :] += sums[p] * weight[0:1, :]
                put_halves(rhs, z.padded, first, p * e, full_rows(sums[p], 16))

        by_groups(z, group)
        return carry

    lax.fori_loop(1, DERIVATIVES, derivative, 0)
    for q in range(z.quantities):
        for first, rows in z.groups():
            put_halves(moments, z.padded, first, q * e, full_rows(total[q, first : first + rows, :], 16))


def along_lanes(blocks, wanted, elements):
    face, lane = wanted >> (elements.bit_length() - 1), wanted & (elements - 1)
    result = []
    for rows in zip(*blocks):
        picked = jnp.zeros_like(rows[0])
        for j, row in enumerate(rows):
            shape = row.shape
            taken = jnp.take_along_axis(row, jnp.broadcast_to(lane, shape), axis=1, mode="promise_in_bounds")
            picked = jnp.where(jnp.broadcast_to(face == j, shape), taken, picked)
        result.append(picked)
    return result


def dense_rows(z, target, value):
    for q in range(z.quantities):
        target[q * z.face_basis : q * z.face_basis + z.face_rows, :] = value[q * z.face_rows : (q + 1) * z.face_rows]


def send_kernel(z, moments, project, send_hot, send_last, *refs):
    count = len(z.plan)
    outgoing = refs[:count]
    table, faces = refs[count:]
    e, r, half = z.elements, z.face_rows, z.block_padded
    projected = product(project[...], moments[...])
    faces[...] = projected
    blocks = []
    for j in range(z.faces):
        pieces = [projected[j * r : (j + 1) * r, q * e : (q + 1) * e] for q in range(z.quantities)]
        blocks.append([piece[k : k + 8] for piece in pieces for k in range(0, r, 8)])
        high, low = halves(full_rows(jnp.concatenate(pieces, axis=0), half))
        table[:half, j * e : (j + 1) * e] = high
        table[half:, j * e : (j + 1) * e] = low
    by_product = z.by_product
    if by_product:
        picked = product(table[...], send_hot[...])
        for t in range(by_product):
            columns = slice(t * z.slots, (t + 1) * z.slots)
            dense_rows(z, outgoing[t], picked[: z.block, columns] + picked[half : half + z.block, columns])
    for t in range(by_product, count):
        rows = along_lanes(blocks, send_last[t - by_product : t - by_product + 1, :], e)
        dense_rows(z, outgoing[t], jnp.concatenate(rows, axis=0))


def first_kernel(z, *refs):
    given = refs[:8]
    state, jacobians, cluster, turns, stiff, project, send_hot, send_last, weights = refs[8:17]
    wide_stiff, wide_project, stiffness, projection, lists, sizes, arrived = refs[17:]
    targets = [state, jacobians, stiffness, projection, cluster, turns, lists, sizes]
    copies = [pltpu.make_async_copy(given[n], targets[n], arrived.at[n]) for n in range(8)]
    for n in (6, 7, 2, 3, 4, 5, 0, 1):
        copies[n].start()
    for n in (6, 7):
        copies[n].wait()
    slot = lax.broadcasted_iota(jnp.int32, (1, z.slots), 1)
    for t, entry in enumerate(z.plan):
        chosen = lists_of(entry)[0]
        wanted = jnp.where(slot < sizes[0, chosen], lists[pl.ds(chosen, 1), :], -1)
        if t < z.by_product:
            send_hot[:, t * z.slots : (t + 1) * z.slots] = one_hot((z.face_total, z.slots), wanted, 0)
        else:
            send_last[t - z.by_product : t - z.by_product + 1, :] = wanted
    for n in (2, 3, 4):
        copies[n].wait()
    weight_rows(z, 0, cluster, weights)
    stiff[...] = left_parts(wide_stiff, stiffness_rows(z, stiffness, -1.0), z.padded)
    project[...] = left_parts(
        wide_project, [(j * z.face_rows, 0, projection[:, j, :]) for j in range(z.faces)], z.padded
    )
    for n in (5, 0, 1):
        copies[n].wait()


def tables_kernel(z, *refs):
    volume, lift, rotation, neighbours, orient = refs[:5]
    volume_left, lift_left, turned_left, picks, own_hot, far_hot, last_hot = refs[5:12]
    wide_volume, wide_lift, wide_turned = refs[12:]
    e, r, f = z.elements, z.face_rows, z.face_basis
    volume_left[...] = left_parts(wide_volume, stiffness_rows(z, volume, 1.0), z.padded)
    plain, turned = [], []
    for i in range(z.faces):
        face = jnp.transpose(lift[:, i, :], (1, 0))
        plain.append((0, i * r, face))
        for o in range(z.rotations):
            value = jnp.dot(face, rotation[o], precision=lax.Precision.HIGHEST, preferred_element_type=F32)
            turned.append((0, o * z.lifted + i * r, value))
    lift_left[...] = left_parts(wide_lift, plain, z.lifted)
    wide_turned[...] = jnp.zeros_like(wide_turned)
    for row, column, value in turned:
        high = value.astype(BF16).astype(F32)
        columns = slice(column, column + value.shape[1])
        wide_turned[: z.basis, columns] = high
        wide_turned[z.basis :, columns] = value - high
    turned_left[...] = wide_turned[...].astype(BF16)
    for o in range(z.rotations):
        rows = [
            jnp.broadcast_to(jnp.where(orient[i : i + 1, :] == o, 1.0, 0.0), (r, e)) for i in range(z.faces)
        ]
        picks[o] = jnp.concatenate(rows, axis=0).astype(BF16)
    for i in range(z.faces):
        wanted = neighbours[i : i + 1, :]
        own_hot[:, i * e : (i + 1) * e] = one_hot((z.face_total, e), wanted, 0)
        for t, entry in enumerate(z.plan):
            _, direction, exists = lists_of(entry)
            offset = jnp.where(exists, z.face_total + direction * z.slots, -z.slots)
            hot = one_hot((z.slots, e), wanted, offset)
            if t >= z.early:
                row = (t - z.early) * z.slots
                last_hot[row : row + z.slots, i * e : (i + 1) * e] = hot
            else:
                far_hot[t * z.slots : (t + 1) * z.slots, i * e : (i + 1) * e] = hot


def solve(z, index, block, solver, store):
    together = 2 if z.faces % 2 == 0 else 1
    for i in range(0, z.faces, together):
        sums = [[None] * together for _ in range(z.chunk)]
        for q in range(z.quantities):
            for j in range(together):
                value = block(q, i + j)
                for c in range(z.chunk):
                    term = value * solver[q, index * z.chunk + c, i + j : i + j + 1, :]
                    sums[c][j] = term if sums[c][j] is None else sums[c][j] + term
        for c in range(z.chunk):
            column = (index * z.chunk + c) * z.elements
            if not isinstance(column, int):
                column = pl.multiple_of(column, z.elements)
            store(i, together, column, sums[c])


def inner_kernel(z, running, table, faces, moments, jacobians, local_solver, volume_left, lift_left, own_hot, gathered, partial, mixed, rhs):
    e, r = z.elements, z.face_rows
    picked = product(table[...], own_hot[...])
    gathered[...] = picked[: z.block, :] + picked[z.block_padded : z.block_padded + z.block, :]
    def store(i, j, p, values):
        put_halves(rhs, z.lifted, i * r, p, jnp.concatenate(values, axis=0))

    def some(index, carry):
        solve(z, index, lambda q, i: faces[i * r : (i + 1) * r, q * e : (q + 1) * e], local_solver, store)
        return carry

    lax.fori_loop(0, z.quantities // z.chunk, some, 0)
    lifted = product(lift_left[...], rhs[...])
    for q in range(z.quantities):
        partial[q] = running[q] - lifted[:, q * e : (q + 1) * e]
    mixed[...] = product(volume_left[...], moments[...])

    def group(first, rows):
        sums = contract(z, mixed, jacobians, first, rows)
        for p in range(z.quantities):
            partial[p, pl.ds(first, rows), :] += sums[p]

    by_groups(z, group)


def received_blocks(z, incoming, gathered, far_hot, received):
    b, half = z.block, z.block_padded
    for t, source in enumerate(incoming):
        pieces = [source[q * z.face_basis : q * z.face_basis + z.face_rows, :] for q in range(z.quantities)]
        high, low = halves(full_rows(jnp.concatenate(pieces, axis=0), half))
        received[:half, t * z.slots : (t + 1) * z.slots] = high
        received[half:, t * z.slots : (t + 1) * z.slots] = low
    picked = product(received[...], far_hot[...])
    return gathered[...] + picked[:b, :] + picked[half : half + b, :]


def early_kernel(z, *refs):
    *incoming, gathered, far_hot, blocks, received = refs
    blocks[...] = received_blocks(z, incoming, gathered, far_hot, received)


def neighbour_flux(z, incoming, gathered, neighbour_solver, picks, far_hot, turned_left, received, blocks, turned, take):
    e, r, b = z.elements, z.face_rows, z.basis
    blocks[...] = received_blocks(z, incoming, gathered, far_hot, received)
    width = z.rotations * z.lifted

    def store(i, together, column, values):
        high, low = halves(jnp.concatenate(values, axis=0))
        rows = together * r
        for o in range(z.rotations):
            pick = picks[o, i * r : i * r + rows, :]
            row = o * z.lifted + i * r
            turned[row : row + rows, pl.ds(column, e)] = high * pick
            turned[width + row : width + row + rows, pl.ds(column, e)] = low * pick

    for index in range(z.quantities // z.chunk):
        solve(z, index, lambda q, i: blocks[q * r : (q + 1) * r, i * e : (i + 1) * e], neighbour_solver, store)
    both = product(turned_left[...], turned[:width, :])
    flux = both[:b, :] + both[b:, :] + product(turned_left[:b, :], turned[width:, :])
    for q in range(z.quantities):
        take(q, flux[:, q * e : (q + 1) * e])


def flux_kernel(z, substep, *refs):
    incoming, refs = refs[: z.late], refs[z.late :]
    gathered, partial, solution, neighbour_solver, picks, far_hot, turned_left, cluster = refs[:8]
    updated, running, weights, received, blocks, turned = refs[8:]
    weight_rows(z, substep + 1, cluster, weights)
    ending = ((substep + 1) & (period_of(cluster[...]) - 1)) == 0

    def take(q, flux):
        value = partial[q] - flux
        running[q] = value
        updated[q] = jnp.where(ending, value, solution[q])

    neighbour_flux(
        z, incoming, gathered, neighbour_solver, picks, far_hot, turned_left, received, blocks, turned, take
    )


def last_kernel(z, *refs):
    incoming, refs = refs[: z.late], refs[z.late :]
    gathered, partial, neighbour_solver, picks, far_hot, turned_left = refs[:6]
    advanced, received, blocks, turned, done, sent = refs[6:]
    groups = z.quantities // z.chunk

    def copy(index):
        part = pl.ds(index * z.chunk, z.chunk)
        return pltpu.make_async_copy(done.at[part], advanced.at[part], sent.at[index])

    def take(q, flux):
        done[q] = partial[q] - flux

    neighbour_flux(
        z, incoming, gathered, neighbour_solver, picks, far_hot, turned_left, received, blocks, turned, take
    )
    for index in range(groups):
        copy(index).start()
    for index in range(groups):
        copy(index).wait()


def call(body, outs, scratch, cost, arguments, space=pltpu.VMEM, out_space=pltpu.VMEM, more=(), flags=None):
    in_specs = [pl.BlockSpec(memory_space=space)] * len(arguments)
    return pl.pallas_call(
        body,
        out_shape=[jax.ShapeDtypeStruct(shape, kind) for shape, kind in outs],
        in_specs=in_specs,
        out_specs=[pl.BlockSpec(memory_space=out_space)] * len(outs),
        scratch_shapes=[*(pltpu.VMEM(shape, kind) for shape, kind in scratch), *more],
        cost_estimate=pl.CostEstimate(flops=cost, bytes_accessed=1 << 20, transcendentals=0),
        compiler_params=pltpu.CompilerParams(vmem_limit_bytes=24 << 20, flags=flags or {}),
    )(*arguments)


def local(
    plan,
    solution,
    jacobians,
    derivative_stiffness,
    volume_stiffness,
    face_project,
    face_lift,
    face_rotation,
    local_solver,
    neighbour_solver,
    cluster,
    neighbours,
    orient,
    send_faces,
    counts,
):
    z = Sizes(solution, face_project, send_faces, plan)
    count = len(plan)
    sizes = [lax.axis_size(axis) for axis in AXES]
    state = solution.transpose(1, 0, 2)
    jacobians = jacobians.transpose(1, 2, 0, 3)
    local_solver = local_solver.transpose(1, 2, 0, 3)
    neighbour_solver = neighbour_solver.transpose(1, 2, 0, 3)
    projection = face_project.transpose(1, 0, 2)
    lift = face_lift.transpose(2, 0, 1)
    cluster = cluster.reshape(1, -1)
    counts = counts.reshape(1, -1)

    block = (((z.quantities - 1) * z.face_basis + z.face_rows, z.slots), F32)
    table = ((2 * z.block_padded, z.face_total), BF16)
    faces = ((z.lifted, z.columns), F32)
    moments = ((3 * z.padded, z.columns), BF16)
    stiff = ((3 * z.basis, 3 * z.padded), BF16)
    project = ((z.lifted, 3 * z.padded), BF16)
    field = ((z.quantities, z.basis, z.elements), F32)
    gathered = ((z.block, z.face_total), F32)
    send_hot = ((z.face_total, max(1, z.by_product) * z.slots), BF16)
    send_last = ((max(1, count - z.by_product), z.slots), jnp.int32)
    far_hot = ((z.early * z.slots, z.face_total), BF16)
    last_hot = ((z.late * z.slots, z.face_total), BF16)
    own_hot = ((z.face_total, z.face_total), BF16)
    lift_left = ((z.basis, 3 * z.lifted), BF16)
    turned_left = ((2 * z.basis, z.rotations * z.lifted), BF16)
    picks = ((z.rotations, z.lifted, z.elements), BF16)
    mixed = ((3 * z.basis, z.columns), F32)
    weights = ((DERIVATIVES, 8, z.elements), F32)
    received = ((2 * z.block_padded, z.early * z.slots), BF16)
    last_received = ((2 * z.block_padded, z.late * z.slots), BF16)
    turned = ((2 * z.rotations * z.lifted, z.columns), BF16)

    def wide(entry):
        return (entry[0], F32)

    given = (
        state, jacobians, derivative_stiffness, projection, cluster, face_rotation, send_faces, counts,
    )
    results = call(
        functools.partial(first_kernel, z),
        [(given[n].shape, given[n].dtype) for n in (0, 1, 4, 5)] + [stiff, project, send_hot, send_last, weights],
        [wide(stiff), wide(project)],
        1_000_000,
        tuple(pltpu.with_memory_space_constraint(value, pltpu.HBM) for value in given),
        space=pltpu.HBM,
        more=[
            *(pltpu.VMEM(given[n].shape, given[n].dtype) for n in (2, 3, 6)),
            pltpu.SMEM(counts.shape, counts.dtype),
            pltpu.SemaphoreType.DMA((len(given),)),
        ],
    )
    state, jacobians, cluster, turns, stiff_left, project_left, send_matrix, send_rest, weights_now = results
    running = state
    for substep in range(SUBSTEPS):
        (moments_now,) = call(
            functools.partial(predictor_kernel, z),
            [moments],
            [moments, mixed, field],
            10_000_000,
            (state, jacobians, stiff_left, weights_now),
        )
        *outgoing, table_now, faces_now = call(
            functools.partial(send_kernel, z),
            [block] * count + [table, faces],
            [],
            5_000_000,
            (moments_now, project_left, send_matrix, send_rest),
        )
        incoming = [lax.ppermute(value, AXES, partners(sizes, entry)) for value, entry in zip(outgoing, plan)]
        if substep == 0:
            volume_left, lift_plain, lift_turned, orient_picks, own_matrix, far_matrix, last_matrix = call(
                functools.partial(tables_kernel, z),
                [stiff, lift_left, turned_left, picks, own_hot, far_hot, last_hot],
                [wide(stiff), wide(lift_left), wide(turned_left)],
                1_000_000,
                (volume_stiffness, lift, turns, neighbours, orient),
            )
        gathered_now, partial = call(
            functools.partial(inner_kernel, z),
            [gathered, field],
            [mixed, ((3 * z.lifted, z.columns), BF16)],
            10_000_000,
            (running, table_now, faces_now, moments_now, jacobians, local_solver, volume_left, lift_plain, own_matrix),
        )
        (gathered_now,) = call(
            functools.partial(early_kernel, z),
            [gathered],
            [received],
            5_000_000,
            (*incoming[: z.early], gathered_now, far_matrix),
        )
        if substep == SUBSTEPS - 1:
            (advanced,) = call(
                functools.partial(last_kernel, z),
                [field],
                [last_received, gathered, turned, field],
                10_000_000,
                (*incoming[z.early :], gathered_now, partial, neighbour_solver, orient_picks, last_matrix, lift_turned),
                out_space=pltpu.HBM,
                more=[pltpu.SemaphoreType.DMA((z.quantities // z.chunk,))],
            )
            return advanced.transpose(1, 0, 2)
        state, running, weights_now = call(
            functools.partial(flux_kernel, z, substep),
            [field, field, weights],
            [last_received, gathered, turned],
            10_000_000,
            (
                *incoming[z.early :], gathered_now, partial, state, neighbour_solver, orient_picks, last_matrix, lift_turned,
                cluster,
            ),
        )


def solution(mesh):
    spread = ("gx", "gy", "gz")
    return jax.shard_map(
        functools.partial(local, exchange_plan(mesh)),
        mesh=mesh,
        in_specs=(
            P(None, None, spread),
            P(None, None, None, spread),
            P(),
            P(),
            P(),
            P(),
            P(),
            P(None, None, None, spread),
            P(None, None, None, spread),
            P(spread),
            P(None, spread),
            P(None, spread),
            P(None, spread),
            P(None, spread),
        ),
        out_specs=P(None, None, spread),
        check_vma=False,
    )
```

```python
import functools
import math

import jax
import jax.numpy as jnp
from jax import lax
from jax.experimental import pallas as pl
from jax.experimental.pallas import tpu as pltpu
from jax.sharding import PartitionSpec as P

DERIVATIVES = 6
SUBSTEPS = 4
SPAN = 1.0
F32 = jnp.float32
BF16 = jnp.bfloat16
AXES = ("gx", "gy", "gz")


def rounded(size, unit):
    return -(-size // unit) * unit


def halves(value):
    high = value.astype(BF16)
    return high, (value - high.astype(F32)).astype(BF16)


def product(left, right):
    return jnp.dot(left, right, preferred_element_type=F32)


def exchange_plan(mesh):
    plan = []
    for number, axis in enumerate(AXES):
        size = mesh.shape[axis]
        if size == 1:
            continue
        if size == 2:
            plan.append((number, size, "pair0"))
        elif size % 2 == 0:
            plan.append((number, size, "pair0"))
            plan.append((number, size, "pair1"))
        else:
            plan.append((number, size, "up"))
            plan.append((number, size, "down"))
    return tuple(sorted(plan, key=lambda entry: (entry[2] == "pair1", entry[2] == "pair0" and entry[0] != 2)))


def partners(sizes, entry):
    number, size, kind = entry
    spare = [other for other in (2, 0, 1) if other != number and sizes[other] % 2 == 0]
    pairs = []
    for flat in range(math.prod(sizes)):
        place = [flat // (sizes[1] * sizes[2]), flat // sizes[2] % sizes[1], flat % sizes[2]]
        source = flat
        here = place[number]
        if kind in ("up", "down"):
            place[number] = (here + (1 if kind == "up" else -1)) % size
        elif kind == "pair0":
            place[number] = here ^ 1
        elif 0 < here < size - 1:
            place[number] = ((here + 1) ^ 1) - 1
        elif spare:
            place[spare[0]] ^= 1
        else:
            place[number] = size - 1 - here
        pairs.append((source, (place[0] * sizes[1] + place[1]) * sizes[2] + place[2]))
    return pairs


def lists_of(entry):
    number, size, kind = entry
    place = lax.axis_index(AXES[number])
    if kind == "up":
        return 2 * number, 2 * number, place > 0
    if kind == "down":
        return 2 * number + 1, 2 * number + 1, place < size - 1
    parity = lax.rem(place, 2)
    upper = parity if kind == "pair0" else 1 - parity
    exists = jnp.where(upper == 1, place > 0, place < size - 1)
    return 2 * number + upper, 2 * number + 1 - upper, exists


class Sizes:
    def __init__(self, solution, face_project, send_faces, plan):
        self.basis, self.quantities, self.elements = solution.shape
        self.faces, self.face_basis, _ = face_project.shape
        self.slots = send_faces.shape[1]
        self.plan = plan
        self.padded = rounded(self.basis, 16)
        self.face_rows = rounded(self.face_basis, 8)
        self.block = self.quantities * self.face_rows
        self.block_padded = rounded(self.block, 16)
        self.columns = self.quantities * self.elements
        self.face_total = self.faces * self.elements
        self.lifted = self.faces * self.face_rows
        self.rotations = 3
        count = len(plan)
        self.by_product = count - 1 if count % 2 and count > 1 and self.elements == 128 else count
        self.late = min(2, count - 1) if count > 1 else 0
        self.early = count - self.late
        self.chunk = 3 if self.quantities % 3 == 0 else 1

    def groups(self):
        return [(k, min(16, self.basis - k)) for k in range(0, self.basis, 16)]


def left_parts(scratch, pieces, width):
    scratch[...] = jnp.zeros_like(scratch)
    for row, column, value in pieces:
        high = value.astype(BF16).astype(F32)
        rows, columns = value.shape
        scratch[row : row + rows, column : column + columns] = high
        scratch[row : row + rows, width + column : width + column + columns] = high
        scratch[row : row + rows, 2 * width + column : 2 * width + column + columns] = value - high
    return scratch[...].astype(BF16)


def stiffness_rows(z, matrices, sign):
    pieces = []
    for first, rows in z.groups():
        for d in range(3):
            pieces.append((3 * first + d * rows, 0, sign * matrices[d, first : first + rows, :]))
    return pieces


def one_hot(shape, targets, offset):
    rows = lax.broadcasted_iota(jnp.int32, shape, 0)
    return jnp.where(rows == targets - offset, 1.0, 0.0).astype(BF16)


def period_of(cluster):
    return jnp.left_shift(jnp.ones_like(cluster), cluster)


def weights_of(cluster, substep):
    offset = (substep & (period_of(cluster) - 1)).astype(F32)
    step = SPAN / SUBSTEPS
    upper, lower = (offset + 1.0) * step, offset * step
    rows, high, low = [], upper, lower
    for power in range(DERIVATIVES):
        rows.append((high - low) * (1.0 / math.factorial(power + 1)))
        high, low = high * upper, low * lower
    return rows


def put_halves(target, width, row, column, value):
    high, low = halves(value)
    rows, columns = value.shape
    for part, piece in enumerate((high, low, high)):
        start = part * width + row
        if not isinstance(row, int):
            start = pl.multiple_of(start, 16)
        target[pl.ds(start, rows), pl.ds(column, columns)] = piece


def by_groups(z, group):
    whole = z.basis // 16
    group(0, 16)

    def later(index, carry):
        group(pl.multiple_of(index * 16, 16), 16)
        return carry

    lax.fori_loop(1, whole, later, 0)
    if z.basis % 16:
        group(whole * 16, z.basis % 16)


def contract(z, mixed, jacobians, first, rows):
    totals = [None] * z.quantities
    for q in range(z.quantities):
        for d in range(3):
            start = 3 * first + d * rows
            if not isinstance(first, int):
                start = pl.multiple_of(start, 16)
            value = mixed[pl.ds(start, rows), q * z.elements : (q + 1) * z.elements]
            for p in range(z.quantities):
                term = value * jacobians[q, p, d : d + 1, :]
                totals[p] = term if totals[p] is None else totals[p] + term
    return totals


def full_rows(value, rows):
    short = rows - value.shape[0]
    if short == 0:
        return value
    return jnp.concatenate([value, jnp.zeros((short, value.shape[1]), value.dtype)], axis=0)


def weight_rows(z, substep, cluster, weights):
    for power, row in enumerate(weights_of(cluster[...], substep)):
        weights[power] = jnp.broadcast_to(row, (8, z.elements))


def predictor_kernel(z, state, jacobians, stiff, weights, moments, rhs, mixed, total):
    e = z.elements
    for q in range(z.quantities):
        for first, rows in z.groups():
            value = state[q, first : first + rows, :]
            total[q, first : first + rows, :] = value * weights[0, 0:1, :]
            put_halves(rhs, z.padded, first, q * e, full_rows(value, 16))

    def derivative(power, carry):
        mixed[...] = product(stiff[...], rhs[...])
        weight = weights[power]

        def group(first, rows):
            sums = contract(z, mixed, jacobians, first, rows)
            for p in range(z.quantities):
                total[p, pl.ds(first, rows), :] += sums[p] * weight[0:1, :]
                put_halves(rhs, z.padded, first, p * e, full_rows(sums[p], 16))

        by_groups(z, group)
        return carry

    lax.fori_loop(1, DERIVATIVES, derivative, 0)
    for q in range(z.quantities):
        for first, rows in z.groups():
            put_halves(moments, z.padded, first, q * e, full_rows(total[q, first : first + rows, :], 16))


def along_lanes(blocks, wanted, elements):
    face, lane = wanted >> (elements.bit_length() - 1), wanted & (elements - 1)
    result = []
    for rows in zip(*blocks):
        picked = jnp.zeros_like(rows[0])
        for j, row in enumerate(rows):
            shape = row.shape
            taken = jnp.take_along_axis(row, jnp.broadcast_to(lane, shape), axis=1, mode="promise_in_bounds")
            picked = jnp.where(jnp.broadcast_to(face == j, shape), taken, picked)
        result.append(picked)
    return result


def dense_rows(z, target, value):
    for q in range(z.quantities):
        target[q * z.face_basis : q * z.face_basis + z.face_rows, :] = value[q * z.face_rows : (q + 1) * z.face_rows]


def send_kernel(z, moments, project, send_hot, send_last, *refs):
    count = len(z.plan)
    outgoing = refs[:count]
    table, faces = refs[count:]
    e, r, half = z.elements, z.face_rows, z.block_padded
    projected = product(project[...], moments[...])
    faces[...] = projected
    blocks = []
    for j in range(z.faces):
        pieces = [projected[j * r : (j + 1) * r, q * e : (q + 1) * e] for q in range(z.quantities)]
        blocks.append([piece[k : k + 8] for piece in pieces for k in range(0, r, 8)])
        high, low = halves(full_rows(jnp.concatenate(pieces, axis=0), half))
        table[:half, j * e : (j + 1) * e] = high
        table[half:, j * e : (j + 1) * e] = low
    by_product = z.by_product
    if by_product:
        picked = product(table[...], send_hot[...])
        for t in range(by_product):
            columns = slice(t * z.slots, (t + 1) * z.slots)
            dense_rows(z, outgoing[t], picked[: z.block, columns] + picked[half : half + z.block, columns])
    for t in range(by_product, count):
        rows = along_lanes(blocks, send_last[t - by_product : t - by_product + 1, :], e)
        dense_rows(z, outgoing[t], jnp.concatenate(rows, axis=0))


def first_kernel(z, *refs):
    given = refs[:8]
    state, jacobians, cluster, turns, stiff, project, send_hot, send_last, weights = refs[8:17]
    wide_stiff, wide_project, stiffness, projection, lists, sizes, arrived = refs[17:]
    targets = [state, jacobians, stiffness, projection, cluster, turns, lists, sizes]
    copies = [pltpu.make_async_copy(given[n], targets[n], arrived.at[n]) for n in range(8)]
    for n in (6, 7, 2, 3, 4, 5, 0, 1):
        copies[n].start()
    for n in (6, 7):
        copies[n].wait()
    slot = lax.broadcasted_iota(jnp.int32, (1, z.slots), 1)
    for t, entry in enumerate(z.plan):
        chosen = lists_of(entry)[0]
        wanted = jnp.where(slot < sizes[0, chosen], lists[pl.ds(chosen, 1), :], -1)
        if t < z.by_product:
            send_hot[:, t * z.slots : (t + 1) * z.slots] = one_hot((z.face_total, z.slots), wanted, 0)
        else:
            send_last[t - z.by_product : t - z.by_product + 1, :] = wanted
    for n in (2, 3, 4):
        copies[n].wait()
    weight_rows(z, 0, cluster, weights)
    stiff[...] = left_parts(wide_stiff, stiffness_rows(z, stiffness, -1.0), z.padded)
    project[...] = left_parts(
        wide_project, [(j * z.face_rows, 0, projection[:, j, :]) for j in range(z.faces)], z.padded
    )
    for n in (5, 0, 1):
        copies[n].wait()


def tables_kernel(z, *refs):
    volume, lift, rotation, neighbours, orient = refs[:5]
    volume_left, lift_left, turned_left, picks, own_hot, far_hot, last_hot = refs[5:12]
    wide_volume, wide_lift, wide_turned = refs[12:]
    e, r, f = z.elements, z.face_rows, z.face_basis
    volume_left[...] = left_parts(wide_volume, stiffness_rows(z, volume, 1.0), z.padded)
    plain, turned = [], []
    for i in range(z.faces):
        face = jnp.transpose(lift[:, i, :], (1, 0))
        plain.append((0, i * r, face))
        for o in range(z.rotations):
            value = jnp.dot(face, rotation[o], precision=lax.Precision.HIGHEST, preferred_element_type=F32)
            turned.append((0, o * z.lifted + i * r, value))
    lift_left[...] = left_parts(wide_lift, plain, z.lifted)
    wide_turned[...] = jnp.zeros_like(wide_turned)
    for row, column, value in turned:
        high = value.astype(BF16).astype(F32)
        columns = slice(column, column + value.shape[1])
        wide_turned[: z.basis, columns] = high
        wide_turned[z.basis :, columns] = value - high
    turned_left[...] = wide_turned[...].astype(BF16)
    for o in range(z.rotations):
        rows = [
            jnp.broadcast_to(jnp.where(orient[i : i + 1, :] == o, 1.0, 0.0), (r, e)) for i in range(z.faces)
        ]
        picks[o] = jnp.concatenate(rows, axis=0).astype(BF16)
    for i in range(z.faces):
        wanted = neighbours[i : i + 1, :]
        own_hot[:, i * e : (i + 1) * e] = one_hot((z.face_total, e), wanted, 0)
        for t, entry in enumerate(z.plan):
            _, direction, exists = lists_of(entry)
            offset = jnp.where(exists, z.face_total + direction * z.slots, -z.slots)
            hot = one_hot((z.slots, e), wanted, offset)
            if t >= z.early:
                row = (t - z.early) * z.slots
                last_hot[row : row + z.slots, i * e : (i + 1) * e] = hot
            else:
                far_hot[t * z.slots : (t + 1) * z.slots, i * e : (i + 1) * e] = hot


def solve(z, index, block, solver, store):
    together = 2 if z.faces % 2 == 0 else 1
    for i in range(0, z.faces, together):
        sums = [[None] * together for _ in range(z.chunk)]
        for q in range(z.quantities):
            for j in range(together):
                value = block(q, i + j)
                for c in range(z.chunk):
                    term = value * solver[q, index * z.chunk + c, i + j : i + j + 1, :]
                    sums[c][j] = term if sums[c][j] is None else sums[c][j] + term
        for c in range(z.chunk):
            column = (index * z.chunk + c) * z.elements
            if not isinstance(column, int):
                column = pl.multiple_of(column, z.elements)
            store(i, together, column, sums[c])


def inner_kernel(z, running, table, faces, moments, jacobians, local_solver, volume_left, lift_left, own_hot, gathered, partial, mixed, rhs):
    e, r = z.elements, z.face_rows
    picked = product(table[...], own_hot[...])
    gathered[...] = picked[: z.block, :] + picked[z.block_padded : z.block_padded + z.block, :]
    def store(i, j, p, values):
        put_halves(rhs, z.lifted, i * r, p, jnp.concatenate(values, axis=0))

    def some(index, carry):
        solve(z, index, lambda q, i: faces[i * r : (i + 1) * r, q * e : (q + 1) * e], local_solver, store)
        return carry

    lax.fori_loop(0, z.quantities // z.chunk, some, 0)
    lifted = product(lift_left[...], rhs[...])
    for q in range(z.quantities):
        partial[q] = running[q] - lifted[:, q * e : (q + 1) * e]
    mixed[...] = product(volume_left[...], moments[...])

    def group(first, rows):
        sums = contract(z, mixed, jacobians, first, rows)
        for p in range(z.quantities):
            partial[p, pl.ds(first, rows), :] += sums[p]

    by_groups(z, group)


def received_blocks(z, incoming, gathered, far_hot, received):
    b, half = z.block, z.block_padded
    for t, source in enumerate(incoming):
        pieces = [source[q * z.face_basis : q * z.face_basis + z.face_rows, :] for q in range(z.quantities)]
        high, low = halves(full_rows(jnp.concatenate(pieces, axis=0), half))
        received[:half, t * z.slots : (t + 1) * z.slots] = high
        received[half:, t * z.slots : (t + 1) * z.slots] = low
    picked = product(received[...], far_hot[...])
    return gathered[...] + picked[:b, :] + picked[half : half + b, :]


def early_kernel(z, *refs):
    *incoming, gathered, far_hot, blocks, received = refs
    blocks[...] = received_blocks(z, incoming, gathered, far_hot, received)


def neighbour_flux(z, incoming, gathered, neighbour_solver, picks, far_hot, turned_left, received, blocks, turned, take, parts=()):
    e, r, b = z.elements, z.face_rows, z.basis
    blocks[...] = received_blocks(z, incoming, gathered, far_hot, received)
    width = z.rotations * z.lifted

    def store(i, together, column, values):
        high, low = halves(jnp.concatenate(values, axis=0))
        rows = together * r
        for o in range(z.rotations):
            pick = picks[o, i * r : i * r + rows, :]
            row = o * z.lifted + i * r
            turned[row : row + rows, pl.ds(column, e)] = high * pick
            turned[width + row : width + row + rows, pl.ds(column, e)] = low * pick

    for index in range(z.quantities // z.chunk):
        solve(z, index, lambda q, i: blocks[q * r : (q + 1) * r, i * e : (i + 1) * e], neighbour_solver, store)
    for first, last in parts or [(0, z.quantities)]:
        columns = slice(first * e, last * e)
        both = product(turned_left[...], turned[:width, columns])
        flux = both[:b, :] + both[b:, :] + product(turned_left[:b, :], turned[width:, columns])
        for q in range(first, last):
            take(q, flux[:, (q - first) * e : (q - first + 1) * e])


def flux_kernel(z, substep, *refs):
    incoming, refs = refs[: z.late], refs[z.late :]
    gathered, partial, solution, neighbour_solver, picks, far_hot, turned_left, cluster = refs[:8]
    updated, running, weights, received, blocks, turned = refs[8:]
    weight_rows(z, substep + 1, cluster, weights)
    ending = ((substep + 1) & (period_of(cluster[...]) - 1)) == 0

    def take(q, flux):
        value = partial[q] - flux
        running[q] = value
        updated[q] = jnp.where(ending, value, solution[q])

    neighbour_flux(
        z, incoming, gathered, neighbour_solver, picks, far_hot, turned_left, received, blocks, turned, take
    )


def last_kernel(z, *refs):
    incoming, refs = refs[: z.late], refs[z.late :]
    gathered, partial, neighbour_solver, picks, far_hot, turned_left = refs[:6]
    advanced, received, blocks, turned, done, sent = refs[6:]
    middle = z.quantities // 4 * 2
    parts = [(0, middle), (middle, z.quantities)]
    copies = [
        pltpu.make_async_copy(done.at[first:last], advanced.at[first:last], sent.at[n])
        for n, (first, last) in enumerate(parts)
    ]

    def take(q, flux):
        done[q] = partial[q] - flux
        for n, (_, last) in enumerate(parts):
            if q == last - 1:
                copies[n].start()

    neighbour_flux(
        z, incoming, gathered, neighbour_solver, picks, far_hot, turned_left, received, blocks, turned, take, parts
    )
    for copy in copies:
        copy.wait()


def call(body, outs, scratch, cost, arguments, space=pltpu.VMEM, out_space=pltpu.VMEM, more=(), flags=None):
    in_specs = [pl.BlockSpec(memory_space=space)] * len(arguments)
    return pl.pallas_call(
        body,
        out_shape=[jax.ShapeDtypeStruct(shape, kind) for shape, kind in outs],
        in_specs=in_specs,
        out_specs=[pl.BlockSpec(memory_space=out_space)] * len(outs),
        scratch_shapes=[*(pltpu.VMEM(shape, kind) for shape, kind in scratch), *more],
        cost_estimate=pl.CostEstimate(flops=cost, bytes_accessed=1 << 20, transcendentals=0),
        compiler_params=pltpu.CompilerParams(vmem_limit_bytes=24 << 20, flags=flags or {}),
    )(*arguments)


def local(
    plan,
    solution,
    jacobians,
    derivative_stiffness,
    volume_stiffness,
    face_project,
    face_lift,
    face_rotation,
    local_solver,
    neighbour_solver,
    cluster,
    neighbours,
    orient,
    send_faces,
    counts,
):
    z = Sizes(solution, face_project, send_faces, plan)
    count = len(plan)
    sizes = [lax.axis_size(axis) for axis in AXES]
    state = solution.transpose(1, 0, 2)
    jacobians = jacobians.transpose(1, 2, 0, 3)
    local_solver = local_solver.transpose(1, 2, 0, 3)
    neighbour_solver = neighbour_solver.transpose(1, 2, 0, 3)
    projection = face_project.transpose(1, 0, 2)
    lift = face_lift.transpose(2, 0, 1)
    cluster = cluster.reshape(1, -1)
    counts = counts.reshape(1, -1)

    block = (((z.quantities - 1) * z.face_basis + z.face_rows, z.slots), F32)
    table = ((2 * z.block_padded, z.face_total), BF16)
    faces = ((z.lifted, z.columns), F32)
    moments = ((3 * z.padded, z.columns), BF16)
    stiff = ((3 * z.basis, 3 * z.padded), BF16)
    project = ((z.lifted, 3 * z.padded), BF16)
    field = ((z.quantities, z.basis, z.elements), F32)
    gathered = ((z.block, z.face_total), F32)
    send_hot = ((z.face_total, max(1, z.by_product) * z.slots), BF16)
    send_last = ((max(1, count - z.by_product), z.slots), jnp.int32)
    far_hot = ((z.early * z.slots, z.face_total), BF16)
    last_hot = ((z.late * z.slots, z.face_total), BF16)
    own_hot = ((z.face_total, z.face_total), BF16)
    lift_left = ((z.basis, 3 * z.lifted), BF16)
    turned_left = ((2 * z.basis, z.rotations * z.lifted), BF16)
    picks = ((z.rotations, z.lifted, z.elements), BF16)
    mixed = ((3 * z.basis, z.columns), F32)
    weights = ((DERIVATIVES, 8, z.elements), F32)
    received = ((2 * z.block_padded, z.early * z.slots), BF16)
    last_received = ((2 * z.block_padded, z.late * z.slots), BF16)
    turned = ((2 * z.rotations * z.lifted, z.columns), BF16)

    def wide(entry):
        return (entry[0], F32)

    given = (
        state, jacobians, derivative_stiffness, projection, cluster, face_rotation, send_faces, counts,
    )
    results = call(
        functools.partial(first_kernel, z),
        [(given[n].shape, given[n].dtype) for n in (0, 1, 4, 5)] + [stiff, project, send_hot, send_last, weights],
        [wide(stiff), wide(project)],
        1_000_000,
        tuple(pltpu.with_memory_space_constraint(value, pltpu.HBM) for value in given),
        space=pltpu.HBM,
        more=[
            *(pltpu.VMEM(given[n].shape, given[n].dtype) for n in (2, 3, 6)),
            pltpu.SMEM(counts.shape, counts.dtype),
            pltpu.SemaphoreType.DMA((len(given),)),
        ],
    )
    state, jacobians, cluster, turns, stiff_left, project_left, send_matrix, send_rest, weights_now = results
    running = state
    for substep in range(SUBSTEPS):
        (moments_now,) = call(
            functools.partial(predictor_kernel, z),
            [moments],
            [moments, mixed, field],
            10_000_000,
            (state, jacobians, stiff_left, weights_now),
        )
        *outgoing, table_now, faces_now = call(
            functools.partial(send_kernel, z),
            [block] * count + [table, faces],
            [],
            5_000_000,
            (moments_now, project_left, send_matrix, send_rest),
        )
        incoming = [lax.ppermute(value, AXES, partners(sizes, entry)) for value, entry in zip(outgoing, plan)]
        if substep == 0:
            volume_left, lift_plain, lift_turned, orient_picks, own_matrix, far_matrix, last_matrix = call(
                functools.partial(tables_kernel, z),
                [stiff, lift_left, turned_left, picks, own_hot, far_hot, last_hot],
                [wide(stiff), wide(lift_left), wide(turned_left)],
                1_000_000,
                (volume_stiffness, lift, turns, neighbours, orient),
            )
        gathered_now, partial = call(
            functools.partial(inner_kernel, z),
            [gathered, field],
            [mixed, ((3 * z.lifted, z.columns), BF16)],
            10_000_000,
            (running, table_now, faces_now, moments_now, jacobians, local_solver, volume_left, lift_plain, own_matrix),
        )
        (gathered_now,) = call(
            functools.partial(early_kernel, z),
            [gathered],
            [received],
            5_000_000,
            (*incoming[: z.early], gathered_now, far_matrix),
        )
        if substep == SUBSTEPS - 1:
            (advanced,) = call(
                functools.partial(last_kernel, z),
                [field],
                [last_received, gathered, turned, field],
                10_000_000,
                (*incoming[z.early :], gathered_now, partial, neighbour_solver, orient_picks, last_matrix, lift_turned),
                out_space=pltpu.HBM,
                more=[pltpu.SemaphoreType.DMA((2,))],
            )
            return advanced.transpose(1, 0, 2)
        state, running, weights_now = call(
            functools.partial(flux_kernel, z, substep),
            [field, field, weights],
            [last_received, gathered, turned],
            10_000_000,
            (
                *incoming[z.early :], gathered_now, partial, state, neighbour_solver, orient_picks, last_matrix, lift_turned,
                cluster,
            ),
        )


def solution(mesh):
    spread = ("gx", "gy", "gz")
    return jax.shard_map(
        functools.partial(local, exchange_plan(mesh)),
        mesh=mesh,
        in_specs=(
            P(None, None, spread),
            P(None, None, None, spread),
            P(),
            P(),
            P(),
            P(),
            P(),
            P(None, None, None, spread),
            P(None, None, None, spread),
            P(spread),
            P(None, spread),
            P(None, spread),
            P(None, spread),
            P(None, spread),
        ),
        out_specs=P(None, None, spread),
        check_vma=False,
    )
```
